32 devices in a mesh: lat: 8 (over z, x), lon: 4 (over y, core).
Axes of the slice: x: 2, y: 2, z: 4, core: 2. Of those that a mesh axis runs over, the one named last changes fastest.
Arguments:
- field: bfloat16 [69, 256, 2048], P(None, 'lat', 'lon'), may hold values from -6 to 6
- stem_weight: bfloat16 [1104, 512], replicated, may hold values from -0.1875 to 0.1875
- stem_bias: float32 [512], replicated, may hold values from -3 to 3
- token_gain: float32 [512], replicated, may hold values from 0.1 to 1.9
- kv_weight: bfloat16 [512, 1024], replicated, may hold values from -0.25 to 0.25
- latents: float32 [512, 512], replicated, may hold values from -6 to 6
- latent_gain: float32 [512], replicated, may hold values from 0.1 to 1.9
- query_weight: bfloat16 [512, 512], replicated, may hold values from -0.25 to 0.25
- head_gain: float32 [8], replicated, may hold values from 2 to 40
- out_weight: bfloat16 [512, 512], replicated, may hold values from -0.25 to 0.25
- out_gain: float32 [512], replicated, may hold values from 0.1 to 1.9
Outputs:
- tokens: bfloat16 [128, 1024, 512], P('lat', 'lon')
- latent_out: float32 [512, 512], replicated
The draws below stay inside these ranges and needn't reach their ends.
All inputs are finite; a program needn't handle non-finite values.
Results may differ from the reference program's by a relative error of at most 0.015.
The reference program's roundings to bfloat16 on the way count: a program that leaves them out, or rounds other values in their place, can miss the bound.
Values may be sent and summed in bfloat16 or wider, within the bound.
No kernel may reach another device: no remote copies, remote signals or barrier semaphores. Data moves between devices by JAX's collectives and lax.ppermute only.
A program may use at most 512 MiB of HBM per device.

```python
import jax
import jax.numpy as jnp
from jax import lax

CHAN = 69
D = 512
HEADS = 8
HD = 64
LAT = 512
TH = 16
NLAT = 256
NLON = 2048
NTW = 1024
N_LAT = 8


def draw_head_gain(key, part):
    return jnp.exp(jax.random.uniform(key, (HEADS,), jnp.float32, jnp.log(2.0), jnp.log(24.0)))


def steps_of(rng, extent, cuts, smallest, high):
    def one(dim, blocks):
        draws = jax.random.uniform(jax.random.fold_in(jax.random.fold_in(rng, 6), dim), (blocks,), jnp.float32, smallest / len(cuts), high / len(cuts))
        return jnp.repeat(jnp.exp(draws), extent[dim] // blocks).reshape((-1,) + (1,) * (len(extent) - dim - 1))

    level = one(*cuts[0])
    for cut in cuts[1:]:
        level = level * one(*cut)
    return level


def scatter_about(own_key, extent, scale, most, cuts=(), dtype=jnp.bfloat16):
    level = steps_of(own_key, extent, cuts, -0.22, 0.18) if cuts else 1.0
    array = jax.random.normal(own_key, extent, jnp.float32) * scale * level
    return jnp.minimum(jnp.maximum(array, -most), most).astype(dtype)


def setup_inputs(seed: int = 0) -> dict:
    key_of = jax.random.split(jax.random.key(seed), 12)
    field = scatter_about(key_of[0], (CHAN, NLAT, NLON), 1.0, 6.0, ((1, 8), (2, 4)))
    stem_weight = scatter_about(key_of[1], (16 * CHAN, D), (16 * CHAN) ** -0.5, 0.1875)
    stem_bias = scatter_about(key_of[2], (D,), 0.5, 3.0, (), jnp.float32)
    token_gain = jnp.clip(1.0 + 0.18 * jax.random.normal(key_of[3], (D,), jnp.float32), 0.1, 1.9)
    kv_weight = scatter_about(key_of[4], (D, 2 * D), D ** -0.5, 0.25)
    latents = scatter_about(key_of[5], (LAT, D), 1.0, 6.0, (), jnp.float32)
    latent_gain = jnp.clip(1.0 + 0.18 * jax.random.normal(key_of[6], (D,), jnp.float32), 0.1, 1.9)
    query_weight = scatter_about(key_of[7], (D, D), D ** -0.5, 0.25)
    head_gain = draw_head_gain(jax.random.fold_in(key_of[11], 71), 0)
    out_weight = scatter_about(key_of[9], (D, D), D ** -0.5, 0.25)
    out_gain = jnp.clip(1.0 + 0.18 * jax.random.normal(key_of[10], (D,), jnp.float32), 0.1, 1.9)
    return {"field": field, "stem_weight": stem_weight, "stem_bias": stem_bias, "token_gain": token_gain, "kv_weight": kv_weight, "latents": latents, "latent_gain": latent_gain, "query_weight": query_weight, "head_gain": head_gain, "out_weight": out_weight, "out_gain": out_gain}


def normalize(values):
    mean = lax.optimization_barrier(jnp.mean(values, axis=-1, keepdims=True))
    centred = values - mean
    spread = lax.optimization_barrier(jnp.mean(centred * centred, axis=-1, keepdims=True))
    return centred / jnp.sqrt(spread + 1e-05)

def reference(field, stem_weight, stem_bias, token_gain, kv_weight, latents, latent_gain, query_weight, head_gain, out_weight, out_gain):
    widened = jnp.concatenate([field[:, :, -1:], field, field[:, :, :1]], axis=2)
    widened = jnp.pad(widened, ((0, 0), (1, 1), (0, 0)))
    kernel = stem_weight.reshape(4, 4, CHAN, D)
    stem = lax.conv_general_dilated(widened[None], kernel, (2, 2), 'VALID', dimension_numbers=('NCHW', 'HWIO', 'NHWC'), preferred_element_type=jnp.float32)[0]
    tokens = (normalize(stem + stem_bias) * token_gain).astype(jnp.bfloat16)
    normed = (normalize(latents) * latent_gain).astype(jnp.bfloat16)
    query = jnp.dot(normed, query_weight, preferred_element_type=jnp.float32).astype(jnp.bfloat16)
    query_heads = query.reshape(LAT, HEADS, HD).astype(jnp.float32)
    factor = head_gain / jnp.sqrt(jnp.float32(HD))
    bands = tokens.reshape(N_LAT, TH * NTW, D)

    def attend(carry, band):
        peak, total, accum = carry
        kv = jnp.dot(band, kv_weight, preferred_element_type=jnp.float32).astype(jnp.bfloat16)
        keys = kv[:, :D].reshape(-1, HEADS, HD).astype(jnp.float32)
        values = kv[:, D:].reshape(-1, HEADS, HD).astype(jnp.float32)
        scores = jnp.einsum('ihd,thd->hit', query_heads, keys, precision=lax.Precision.HIGHEST) * factor[:, None, None]
        newpeak = jnp.maximum(peak, lax.optimization_barrier(jnp.max(scores, axis=-1)))
        fold = jnp.exp(peak - newpeak)
        expo = jnp.exp(scores - newpeak[:, :, None])
        total = total * fold + lax.optimization_barrier(jnp.sum(expo, axis=-1))
        rounded = expo.astype(jnp.bfloat16).astype(jnp.float32)
        part = jnp.einsum('hit,thd->ihd', rounded, values, precision=lax.Precision.HIGHEST)
        accum = accum * jnp.transpose(fold)[:, :, None] + part
        return ((newpeak, total, accum), None)
    start = (jnp.full((HEADS, LAT), -1e+30, jnp.float32), jnp.zeros((HEADS, LAT), jnp.float32), jnp.zeros((LAT, HEADS, HD), jnp.float32))
    (peak, total, accum), unused = lax.scan(attend, start, bands)
    attended = (accum / jnp.transpose(total)[:, :, None]).reshape(LAT, D).astype(jnp.bfloat16)
    mixed = jnp.dot(attended, out_weight, preferred_element_type=jnp.float32)
    latent_out = normalize(mixed) * out_gain
    return (tokens, latent_out)
```

```python
import functools

import jax
import jax.numpy as jnp
from jax import lax
from jax.experimental import pallas as pl
from jax.experimental.pallas import tpu as pltpu
from jax.sharding import PartitionSpec as P

HEADS = 8
HD = 64
CP = 80
HR = 80
CT = 1024
VMEM = pltpu.VMEM
bf16 = jnp.bfloat16
f32 = jnp.float32
LOG2E = 1.4426950408889634


def call(kernel, out, n_in, scratch=(), smem=0, out_spaces=None):
    outs = out if isinstance(out, (list, tuple)) else [out]
    spaces = out_spaces or [VMEM] * len(outs)
    specs = [pl.BlockSpec(memory_space=s) for s in spaces]
    return pl.pallas_call(
        kernel,
        out_shape=out,
        in_specs=[pl.BlockSpec(memory_space=pltpu.SMEM)] * smem
        + [pl.BlockSpec(memory_space=VMEM)] * n_in,
        out_specs=specs if isinstance(out, (list, tuple)) else specs[0],
        scratch_shapes=list(scratch),
        compiler_params=pltpu.CompilerParams(vmem_limit_bytes=60 << 20),
    )


def shape(dims, dtype):
    return jax.ShapeDtypeStruct(tuple(dims), dtype)


def rows_norm(x, axis):
    mean = jnp.mean(x, axis=axis, keepdims=True)
    centred = x - mean
    spread = jnp.mean(centred * centred, axis=axis, keepdims=True)
    return centred * lax.rsqrt(spread + 1e-05)


def split3(x):
    hi = x.astype(bf16)
    rest = x - hi.astype(f32)
    mid = rest.astype(bf16)
    lo = (rest - mid.astype(f32)).astype(bf16)
    return hi, mid, lo


def query_kernel(gain_ref, latents_ref, lgain_ref, qw_ref, qz_ref):
    normed = (rows_norm(latents_ref[...], 1) * lgain_ref[...]).astype(bf16)
    query = jnp.dot(normed, qw_ref[...], preferred_element_type=f32).astype(bf16)
    qt = jnp.transpose(query.astype(f32))
    zero = jnp.zeros((HD, qt.shape[1]), bf16)
    for h in range(HEADS):
        scaled = qt[h * HD : (h + 1) * HD] * (gain_ref[h] * (LOG2E / HD**0.5))
        hi = scaled.astype(bf16)
        lo = (scaled - hi.astype(f32)).astype(bf16)
        parts = [hi, zero, lo, zero] if h % 2 == 0 else [zero, hi, zero, lo]
        for j, part in enumerate(parts):
            qz_ref[h, j * HD : (j + 1) * HD, :] = part


def encode_kernel(
    place_ref,
    x_ref, hl_ref, hr_ref, top_ref, bot_ref, wt_ref, bias_ref, gain_ref, wk_ref, wvt_ref, qz_ref,
    tok_out, keep_ref, send_ref,
    y_ref, xs_ref, st_ref, tok_ref, k_ref, vt_ref, s_ref, sems,
):
    chan, rows, cols = x_ref.shape
    half = cols // 2
    trows = rows // 2
    width = wk_ref.shape[0]
    tokens = trows * half
    lat = qz_ref.shape[2]

    i = lax.broadcasted_iota(jnp.int32, (256, 256), 0)
    j = lax.broadcasted_iota(jnp.int32, (256, 256), 1)
    perm = jnp.where(((i >> 4) == (j & 15)) & ((i & 15) == (j >> 4)), 1.0, 0.0).astype(bf16)
    for g in range(CP // 16):
        n = min(16, chan - 16 * g)
        for b in range(rows // 16):
            x = x_ref[16 * g : 16 * g + n, 16 * b : 16 * b + 16, :].reshape(n * 16, cols)
            y = jnp.dot(perm[:, : n * 16], x, preferred_element_type=f32).astype(bf16)
            y_ref[1 + 16 * b : 17 + 16 * b, 16 * g : 16 * g + 16, :] = y.reshape(16, 16, cols)
    y_ref[0] = top_ref[:, :cols]
    y_ref[rows + 1] = bot_ref[:, :cols]

    ci = lax.broadcasted_iota(jnp.int32, (cols, cols), 0)
    cj = lax.broadcasted_iota(jnp.int32, (cols, cols), 1)
    want = jnp.where(cj < half, 2 * cj, 2 * (cj - half) + 1)
    select = jnp.where(ci == want, 1.0, 0.0).astype(bf16)
    lane = lax.broadcasted_iota(jnp.int32, (CP, half), 1)
    left_all = hl_ref[...].astype(f32)
    right_all = hr_ref[...].astype(f32)
    edges = [top_ref[:, cols:].astype(f32), bot_ref[:, cols:].astype(f32)]
    for p in range((rows + 2) // 2):
        pair = y_ref[2 * p : 2 * p + 2].reshape(2 * CP, cols)
        sel = jnp.dot(pair, select, preferred_element_type=f32)
        for q in range(2):
            r = 2 * p + q
            if r == 0 or r == rows + 1:
                e = edges[0 if r == 0 else 1]
                left, right = e[:, 0:1], e[:, 1:2]
            else:
                left, right = left_all[:, r - 1 : r], right_all[:, r - 1 : r]
            even = sel[q * CP : (q + 1) * CP, :half]
            odd = sel[q * CP : (q + 1) * CP, half:]
            first = jnp.where(lane == 0, left, pltpu.roll(odd, 1, 1))
            last = jnp.where(lane == half - 1, right, pltpu.roll(even, half - 1, 1))
            for kx, v in enumerate((first, even, odd, last)):
                xs_ref[r, kx * CP : (kx + 1) * CP, :] = v.astype(bf16)

    for h in range(HEADS):
        vt_ref[h * HR + HD : (h + 1) * HR, :] = jnp.ones((HR - HD, tokens), bf16)

    def stem(r, slot):
        patch = xs_ref[pl.ds(2 * r, 4)].reshape(16 * CP, half)
        st_ref[slot] = jnp.dot(wt_ref[...], patch, preferred_element_type=f32)

    def finish(r, slot):
        value = rows_norm(st_ref[slot] + bias_ref[...], 0) * gain_ref[...]
        tt = value.astype(bf16)
        tok = jnp.transpose(tt)
        tok_ref[r] = tok
        pltpu.make_async_copy(tok_ref.at[r], tok_out.at[r], sems.at[r]).start()
        at = pl.ds(pl.multiple_of(r * half, half), half)
        k_ref[at, :] = jnp.dot(tok, wk_ref[...], preferred_element_type=f32).astype(bf16)
        vt = jnp.dot(wvt_ref[...], tt, preferred_element_type=f32).astype(bf16)
        for h in range(HEADS):
            vt_ref[h * HR : h * HR + HD, at] = vt[h * HD : (h + 1) * HD]

    stem(0, 0)

    def band(n, carry):
        r = 2 * n
        stem(r + 1, 1)
        finish(r, 0)
        stem(jnp.minimum(r + 2, trows - 1), 0)
        finish(r + 1, 1)
        return carry

    lax.fori_loop(0, trows // 2, band, 0)

    def produce(h, c, slot):
        pair = pl.ds(pl.multiple_of((h >> 1) * (2 * HD), 2 * HD), 2 * HD)
        keys = k_ref[c * CT : (c + 1) * CT, pair]
        keys = jnp.concatenate([keys, keys], axis=1)
        s = jnp.dot(keys, qz_ref[h], preferred_element_type=f32)
        s_ref[slot] = s
        return jnp.max(s, axis=0, keepdims=True)

    chunks = tokens // CT

    def head_of(t):
        return (t & (HEADS // 2 - 1)) ^ place_ref[t >> (HEADS.bit_length() - 2)]

    def head(t, most):
        h = head_of(t)
        after = head_of(jnp.minimum(t + 1, HEADS - 1))
        peak = jnp.full((1, lat), -1e30, f32)
        state = jnp.zeros((HR, lat), f32)
        for c in range(chunks):
            if c + 1 < chunks:
                following = produce(h, c + 1, (c + 1) % 2)
            else:
                following = produce(after, 0, (c + 1) % 2)
            newpeak = jnp.maximum(peak, jnp.ceil(most))
            fold = jnp.exp2(peak - newpeak)
            weights = jnp.exp2(s_ref[c % 2] - newpeak).astype(bf16)
            values = vt_ref[pl.ds(pl.multiple_of(h * HR, 16), HR), c * CT : (c + 1) * CT]
            state = state * fold + jnp.dot(values, weights, preferred_element_type=f32)
            peak, most = newpeak, following
        total = state[HD : HD + 1]
        packed = pack(state[:HD], total, peak)

        @pl.when(t < HEADS // 2)
        def _():
            keep_ref[jnp.minimum(t, HEADS // 2 - 1)] = packed

        @pl.when(t >= HEADS // 2)
        def _():
            send_ref[jnp.maximum(t - HEADS // 2, 0)] = packed

        return most

    lax.fori_loop(0, HEADS, head, produce(head_of(0), 0, 0))
    for r in range(trows):
        pltpu.make_async_copy(tok_ref.at[r], tok_out.at[r], sems.at[r]).wait()


def pack(sums, total, peak):
    lat = sums.shape[1]
    row = lax.broadcasted_iota(jnp.int32, (16, lat), 0)
    tail = jnp.zeros((16, lat), f32)
    for n, part in enumerate(split3(total) + split3(peak)):
        tail = jnp.where(row == n, part.astype(f32), tail)
    return jnp.concatenate([sums.astype(bf16), tail.astype(bf16)], axis=0)


def unpack(state):
    tail = state[HD:].astype(f32)
    total = (tail[0:1] + tail[1:2]) + tail[2:3]
    peak = (tail[3:4] + tail[4:5]) + tail[5:6]
    return state[:HD].astype(f32), total, peak


def combined(a, b):
    sums_a, total_a, peak_a = unpack(a)
    sums_b, total_b, peak_b = unpack(b)
    peak = jnp.maximum(peak_a, peak_b)
    fold_a = jnp.exp2(peak_a - peak)
    fold_b = jnp.exp2(peak_b - peak)
    return sums_a * fold_a + sums_b * fold_b, total_a * fold_a + total_b * fold_b, peak


def fold_kernel(a_ref, b_ref, *outs):
    per = a_ref.shape[0] // len(outs)
    for n in range(a_ref.shape[0]):
        outs[n // per][n % per] = pack(*combined(a_ref[n], b_ref[n]))


def attended_kernel(a_ref, b_ref, out_ref):
    sums, total, peak = combined(a_ref[0], b_ref[0])
    out_ref[0] = (sums / total).astype(bf16)


def out_kernel(place_ref, a_ref, b_ref, wo_ref, gain_ref, out_ref, all_ref):
    half = HEADS // 2
    for t in range(HEADS):
        value = a_ref[t] if t < half else b_ref[t - half]
        h = (t % half) ^ place_ref[t // half]
        all_ref[pl.ds(pl.multiple_of(h * HD, HD), HD), :] = value.astype(f32)
    attended = jnp.transpose(all_ref[...]).astype(bf16)
    mixed = jnp.dot(attended, wo_ref[...], preferred_element_type=f32)
    out_ref[...] = rows_norm(mixed, 1) * gain_ref[...]


def shards(
    field, stem_weight, stem_bias, token_gain, kv_weight, latents,
    latent_gain, query_weight, head_gain, out_weight, out_gain,
):
    chan, rows, cols = field.shape
    width = stem_weight.shape[1]
    lat = latents.shape[0]
    nlat = lax.axis_size("lat")
    nlon = lax.axis_size("lon")
    half = cols // 2
    trows = rows // 2

    extra = ((0, CP - chan), (0, 0))
    ahead = [(i, (i + 1) % nlon) for i in range(nlon)]
    back = [(t, s) for s, t in ahead]
    hl = lax.ppermute(jnp.pad(field[:, :, cols - 1], extra), "lon", ahead)
    hr = lax.ppermute(jnp.pad(field[:, :, 0], extra), "lon", back)

    def edge(r):
        return jnp.concatenate([jnp.pad(field[:, r, :], extra), hl[:, r : r + 1], hr[:, r : r + 1]], 1)

    up = [(i, i + 1) for i in range(nlat - 1)]
    down = [(t, s) for s, t in up]
    top = lax.ppermute(edge(rows - 1), "lat", up)
    bot = lax.ppermute(edge(0), "lat", down)

    wt = stem_weight.reshape(16, chan, width)
    wt = jnp.pad(wt, ((0, 0), (0, CP - chan), (0, 0))).reshape(16 * CP, width).T
    wk = kv_weight[:, :width]
    wvt = kv_weight[:, width:].T
    qz = call(query_kernel, shape((HEADS, 4 * HD, lat), bf16), 3, smem=1)(
        head_gain, latents, latent_gain[None, :], query_weight
    )

    core = lax.axis_index("lon") & 1
    by = (lax.axis_index("lon") >> 1) & 1
    bx = lax.axis_index("lat") & 1
    yx, xy = 2 * by + bx, 2 * bx + by
    mine = 4 * core + jnp.where(core == 0, yx, xy)
    other = 4 * (1 - core) + jnp.where(core == 0, xy, yx)
    place = jnp.stack([mine, other]).astype(jnp.int32)

    tokens = trows * half
    state = shape((HEADS // 2, HR, lat), bf16)
    tok, keep, send = call(
        encode_kernel,
        [shape((trows, half, width), bf16), state, state],
        11,
        smem=1,
        out_spaces=[pl.ANY, VMEM, VMEM],
        scratch=[
            VMEM((rows + 2, CP, cols), bf16),
            VMEM((rows + 2, 4 * CP, half), bf16),
            VMEM((2, width, half), f32),
            VMEM((trows, half, width), bf16),
            VMEM((tokens, width), bf16),
            VMEM((HEADS * HR, tokens), bf16),
            VMEM((2, CT, lat), f32),
            pltpu.SemaphoreType.DMA((trows,)),
        ],
    )(place, field, hl, hr, top, bot, wt, stem_bias[:, None], token_gain[:, None], wk, wvt, qz)

    def swap(x, flip0, flip1):
        pairs = []
        for a in range(nlat):
            for b in range(nlon):
                axis, bit = flip1 if b & 1 else flip0
                to = (a ^ bit, b) if axis == "lat" else (a, b ^ bit)
                pairs.append((a * nlon + b, to[0] * nlon + to[1]))
        return lax.ppermute(x, ("lat", "lon"), pairs)

    cores = ("lon", 1)
    first, second = ("lon", 2), ("lat", 1)
    rest = [("lat", 1 << n) for n in range(1, nlat.bit_length() - 1)]
    rest += [("lon", 1 << n) for n in range(2, nlon.bit_length() - 1)]

    two = shape((HEADS // 4, HR, lat), bf16)
    one = shape((HEADS // 8, HR, lat), bf16)
    keep, send = call(fold_kernel, [two, two], 2)(keep, swap(send, cores, cores))
    keep, send = call(fold_kernel, [one, one], 2)(keep, swap(send, first, second))
    (mine,) = call(fold_kernel, [one], 2)(keep, swap(send, second, first))
    for n in range(len(rest) - 1):
        (mine,) = call(fold_kernel, [one], 2)(mine, swap(mine, rest[n], rest[(n + 1) % len(rest)]))
    part = call(attended_kernel, shape((1, HD, lat), bf16), 2)(mine, swap(mine, rest[-1], rest[0]))
    part = jnp.concatenate([part, swap(part, second, first)])
    part = jnp.concatenate([part, swap(part, first, second)])
    latent_out = call(
        out_kernel, shape((lat, width), f32), 4, smem=1, scratch=[VMEM((width, lat), f32)]
    )(place, part, swap(part, cores, cores), out_weight, out_gain[None, :])
    return (tok, latent_out)


def solution(mesh):
    return jax.shard_map(
        shards,
        mesh=mesh,
        in_specs=(P(None, "lat", "lon"), P(), P(), P(), P(), P(), P(), P(), P(), P(), P()),
        out_specs=(P("lat", "lon", None), P()),
        check_vma=False,
    )
```

```python
import functools

import jax
import jax.numpy as jnp
from jax import lax
from jax.experimental import pallas as pl
from jax.experimental.pallas import tpu as pltpu
from jax.sharding import PartitionSpec as P

HEADS = 8
HD = 64
CP = 80
HR = 80
CT = 1024
VMEM = pltpu.VMEM
bf16 = jnp.bfloat16
f32 = jnp.float32
LOG2E = 1.4426950408889634


def call(kernel, out, n_in, scratch=(), smem=0, out_spaces=None):
    outs = out if isinstance(out, (list, tuple)) else [out]
    spaces = out_spaces or [VMEM] * len(outs)
    specs = [pl.BlockSpec(memory_space=s) for s in spaces]
    return pl.pallas_call(
        kernel,
        out_shape=out,
        in_specs=[pl.BlockSpec(memory_space=pltpu.SMEM)] * smem
        + [pl.BlockSpec(memory_space=VMEM)] * n_in,
        out_specs=specs if isinstance(out, (list, tuple)) else specs[0],
        scratch_shapes=list(scratch),
        compiler_params=pltpu.CompilerParams(vmem_limit_bytes=60 << 20),
    )


def shape(dims, dtype):
    return jax.ShapeDtypeStruct(tuple(dims), dtype)


def rows_norm(x, axis):
    mean = jnp.mean(x, axis=axis, keepdims=True)
    centred = x - mean
    spread = jnp.mean(centred * centred, axis=axis, keepdims=True)
    return centred * lax.rsqrt(spread + 1e-05)


def split3(x):
    hi = x.astype(bf16)
    rest = x - hi.astype(f32)
    mid = rest.astype(bf16)
    lo = (rest - mid.astype(f32)).astype(bf16)
    return hi, mid, lo


def query_kernel(gain_ref, latents_ref, lgain_ref, qw_ref, qz_ref):
    normed = (rows_norm(latents_ref[...], 1) * lgain_ref[...]).astype(bf16)
    query = jnp.dot(normed, qw_ref[...], preferred_element_type=f32).astype(bf16)
    qt = jnp.transpose(query.astype(f32))
    zero = jnp.zeros((HD, qt.shape[1]), bf16)
    for h in range(HEADS):
        scaled = qt[h * HD : (h + 1) * HD] * (gain_ref[h] * (LOG2E / HD**0.5))
        hi = scaled.astype(bf16)
        lo = (scaled - hi.astype(f32)).astype(bf16)
        parts = [hi, zero, lo, zero] if h % 2 == 0 else [zero, hi, zero, lo]
        for j, part in enumerate(parts):
            qz_ref[h, j * HD : (j + 1) * HD, :] = part


def encode_kernel(
    place_ref,
    x_ref, hl_ref, hr_ref, top_ref, bot_ref, wt_ref, bias_ref, gain_ref, wk_ref, wvt_ref, qz_ref,
    tok_out, keep_ref, send_ref,
    y_ref, xs_ref, st_ref, tok_ref, k_ref, vt_ref, s_ref, col_ref, sems,
):
    chan, rows, cols = x_ref.shape
    half = cols // 2
    trows = rows // 2
    width = wk_ref.shape[0]
    tokens = trows * half
    lat = qz_ref.shape[2]

    i = lax.broadcasted_iota(jnp.int32, (256, 256), 0)
    j = lax.broadcasted_iota(jnp.int32, (256, 256), 1)
    perm = jnp.where(((i >> 4) == (j & 15)) & ((i & 15) == (j >> 4)), 1.0, 0.0).astype(bf16)
    for g in range(CP // 16):
        n = min(16, chan - 16 * g)
        for b in range(rows // 16):
            x = x_ref[16 * g : 16 * g + n, 16 * b : 16 * b + 16, :].reshape(n * 16, cols)
            y = jnp.dot(perm[:, : n * 16], x, preferred_element_type=f32).astype(bf16)
            y_ref[1 + 16 * b : 17 + 16 * b, 16 * g : 16 * g + 16, :] = y.reshape(16, 16, cols)
    y_ref[0] = top_ref[:, :cols]
    y_ref[rows + 1] = bot_ref[:, :cols]

    ci = lax.broadcasted_iota(jnp.int32, (cols, cols), 0)
    cj = lax.broadcasted_iota(jnp.int32, (cols, cols), 1)
    want = jnp.where(cj < half, 2 * cj, 2 * (cj - half) + 1)
    select = jnp.where(ci == want, 1.0, 0.0).astype(bf16)
    lane = lax.broadcasted_iota(jnp.int32, (CP, half), 1)
    left_all = hl_ref[...].astype(f32)
    right_all = hr_ref[...].astype(f32)
    edges = [top_ref[:, cols:].astype(f32), bot_ref[:, cols:].astype(f32)]
    for p in range((rows + 2) // 2):
        pair = y_ref[2 * p : 2 * p + 2].reshape(2 * CP, cols)
        sel = jnp.dot(pair, select, preferred_element_type=f32)
        for q in range(2):
            r = 2 * p + q
            if r == 0 or r == rows + 1:
                e = edges[0 if r == 0 else 1]
                left, right = e[:, 0:1], e[:, 1:2]
            else:
                left, right = left_all[:, r - 1 : r], right_all[:, r - 1 : r]
            even = sel[q * CP : (q + 1) * CP, :half]
            odd = sel[q * CP : (q + 1) * CP, half:]
            first = jnp.where(lane == 0, left, pltpu.roll(odd, 1, 1))
            last = jnp.where(lane == half - 1, right, pltpu.roll(even, half - 1, 1))
            for kx, v in enumerate((first, even, odd, last)):
                xs_ref[r, kx * CP : (kx + 1) * CP, :] = v.astype(bf16)

    for h in range(HEADS):
        vt_ref[h * HR + HD : (h + 1) * HR, :] = jnp.ones((HR - HD, tokens), bf16)

    for n, row in enumerate((bias_ref, gain_ref)):
        col_ref[n] = jnp.transpose(jnp.broadcast_to(row[...], (128, width)))

    def column(n):
        return jnp.concatenate([col_ref[n]] * (half // 128), axis=1)

    def stem(r, slot):
        patch = xs_ref[pl.ds(2 * r, 4)].reshape(16 * CP, half)
        st_ref[slot] = jnp.dot(wt_ref[...], patch, preferred_element_type=f32)

    def finish(r, slot):
        value = rows_norm(st_ref[slot] + column(0), 0) * column(1)
        tt = value.astype(bf16)
        tok = jnp.transpose(tt)
        tok_ref[r] = tok
        pltpu.make_async_copy(tok_ref.at[r], tok_out.at[r], sems.at[r]).start()
        at = pl.ds(pl.multiple_of(r * half, half), half)
        k_ref[at, :] = jnp.dot(tok, wk_ref[...], preferred_element_type=f32).astype(bf16)
        vt = jnp.dot(wvt_ref[...], tt, preferred_element_type=f32).astype(bf16)
        for h in range(HEADS):
            vt_ref[h * HR : h * HR + HD, at] = vt[h * HD : (h + 1) * HD]

    stem(0, 0)

    def band(n, carry):
        r = 2 * n
        stem(r + 1, 1)
        finish(r, 0)
        stem(jnp.minimum(r + 2, trows - 1), 0)
        finish(r + 1, 1)
        return carry

    lax.fori_loop(0, trows // 2, band, 0)

    def produce(h, c, slot):
        pair = pl.ds(pl.multiple_of((h >> 1) * (2 * HD), 2 * HD), 2 * HD)
        keys = k_ref[c * CT : (c + 1) * CT, pair]
        keys = jnp.concatenate([keys, keys], axis=1)
        s = jnp.dot(keys, qz_ref[h], preferred_element_type=f32)
        s_ref[slot] = s
        return jnp.max(s, axis=0, keepdims=True)

    chunks = tokens // CT

    def head_of(t):
        return (t & (HEADS // 2 - 1)) ^ place_ref[t >> (HEADS.bit_length() - 2)]

    def head(t, most):
        h = head_of(t)
        after = head_of(jnp.minimum(t + 1, HEADS - 1))
        peak = jnp.full((1, lat), -1e30, f32)
        state = jnp.zeros((HR, lat), f32)
        for c in range(chunks):
            if c + 1 < chunks:
                following = produce(h, c + 1, (c + 1) % 2)
            else:
                following = produce(after, 0, (c + 1) % 2)
            newpeak = jnp.maximum(peak, jnp.ceil(most))
            fold = jnp.exp2(peak - newpeak)
            weights = jnp.exp2(s_ref[c % 2] - newpeak).astype(bf16)
            values = vt_ref[pl.ds(pl.multiple_of(h * HR, 16), HR), c * CT : (c + 1) * CT]
            state = state * fold + jnp.dot(values, weights, preferred_element_type=f32)
            peak, most = newpeak, following
        total = state[HD : HD + 1]
        packed = pack(state[:HD], total, peak)

        @pl.when(t < HEADS // 2)
        def _():
            keep_ref[jnp.minimum(t, HEADS // 2 - 1)] = packed

        @pl.when(t >= HEADS // 2)
        def _():
            send_ref[jnp.maximum(t - HEADS // 2, 0)] = packed

        return most

    lax.fori_loop(0, HEADS, head, produce(head_of(0), 0, 0))
    for r in range(trows):
        pltpu.make_async_copy(tok_ref.at[r], tok_out.at[r], sems.at[r]).wait()


def pack(sums, total, peak):
    lat = sums.shape[1]
    row = lax.broadcasted_iota(jnp.int32, (16, lat), 0)
    tail = jnp.zeros((16, lat), f32)
    for n, part in enumerate(split3(total) + split3(peak)):
        tail = jnp.where(row == n, part.astype(f32), tail)
    return jnp.concatenate([sums.astype(bf16), tail.astype(bf16)], axis=0)


def unpack(state):
    tail = state[HD:].astype(f32)
    total = (tail[0:1] + tail[1:2]) + tail[2:3]
    peak = (tail[3:4] + tail[4:5]) + tail[5:6]
    return state[:HD].astype(f32), total, peak


def combined(a, b):
    sums_a, total_a, peak_a = a
    sums_b, total_b, peak_b = b
    peak = jnp.maximum(peak_a, peak_b)
    fold_a = jnp.exp2(peak_a - peak)
    fold_b = jnp.exp2(peak_b - peak)
    return sums_a * fold_a + sums_b * fold_b, total_a * fold_a + total_b * fold_b, peak


def fold_kernel(a_ref, b_ref, *outs):
    for n, out in enumerate(outs):
        out[0] = pack(*combined(unpack(a_ref[n]), unpack(b_ref[n])))


def group_kernel(*refs, last):
    states = [unpack(ref[0]) for ref in refs[:-1]]
    while len(states) > 1:
        states = [combined(*states[n : n + 2]) for n in range(0, len(states), 2)]
    sums, total, peak = states[0]
    refs[-1][0] = (sums / total).astype(bf16) if last else pack(sums, total, peak)


def out_kernel(place_ref, *refs):
    parts, (wo_ref, gain_ref, out_ref, all_ref) = refs[:HEADS], refs[HEADS:]
    half = HEADS // 2
    for t in range(HEADS):
        value = parts[t][0]
        h = (t % half) ^ place_ref[t // half]
        all_ref[pl.ds(pl.multiple_of(h * HD, HD), HD), :] = value.astype(f32)
    attended = jnp.transpose(all_ref[...]).astype(bf16)
    mixed = jnp.dot(attended, wo_ref[...], preferred_element_type=f32)
    out_ref[...] = rows_norm(mixed, 1) * gain_ref[...]


def shards(
    field, stem_weight, stem_bias, token_gain, kv_weight, latents,
    latent_gain, query_weight, head_gain, out_weight, out_gain,
):
    chan, rows, cols = field.shape
    width = stem_weight.shape[1]
    lat = latents.shape[0]
    nlat = lax.axis_size("lat")
    nlon = lax.axis_size("lon")
    half = cols // 2
    trows = rows // 2

    extra = ((0, CP - chan), (0, 0))
    ahead = [(i, (i + 1) % nlon) for i in range(nlon)]
    back = [(t, s) for s, t in ahead]
    hl = lax.ppermute(jnp.pad(field[:, :, cols - 1], extra), "lon", ahead)
    hr = lax.ppermute(jnp.pad(field[:, :, 0], extra), "lon", back)

    wt = stem_weight.reshape(16, chan, width)
    wt = jnp.pad(wt, ((0, 0), (0, CP - chan), (0, 0))).reshape(16 * CP, width).T
    wk = kv_weight[:, :width]
    wvt = kv_weight[:, width:].T
    hl, hr, wt, wvt = lax.optimization_barrier((hl, hr, wt, wvt))

    def edge(r):
        return jnp.concatenate([jnp.pad(field[:, r, :], extra), hl[:, r : r + 1], hr[:, r : r + 1]], 1)

    low, high = edge(rows - 1), edge(0)
    low, high, latents = lax.optimization_barrier((low, high, latents))
    up = [(i, i + 1) for i in range(nlat - 1)]
    down = [(t, s) for s, t in up]
    top = lax.ppermute(low, "lat", up)
    bot = lax.ppermute(high, "lat", down)
    qz = call(query_kernel, shape((HEADS, 4 * HD, lat), bf16), 3, smem=1)(
        head_gain, latents, latent_gain[None, :], query_weight
    )

    core = lax.axis_index("lon") & 1
    by = (lax.axis_index("lon") >> 1) & 1
    bx = lax.axis_index("lat") & 1
    yx, xy = 2 * by + bx, 2 * bx + by
    mine = 4 * core + jnp.where(core == 0, yx, xy)
    other = 4 * (1 - core) + jnp.where(core == 0, xy, yx)
    place = jnp.stack([mine, other]).astype(jnp.int32)

    tokens = trows * half
    state = shape((HEADS // 2, HR, lat), bf16)
    tok, keep, send = call(
        encode_kernel,
        [shape((trows, half, width), bf16), state, state],
        11,
        smem=1,
        out_spaces=[pl.ANY, VMEM, VMEM],
        scratch=[
            VMEM((rows + 2, CP, cols), bf16),
            VMEM((rows + 2, 4 * CP, half), bf16),
            VMEM((2, width, half), f32),
            VMEM((trows, half, width), bf16),
            VMEM((tokens, width), bf16),
            VMEM((HEADS * HR, tokens), bf16),
            VMEM((2, CT, lat), f32),
            VMEM((2, width, 128), f32),
            pltpu.SemaphoreType.DMA((trows,)),
        ],
    )(place, field, hl, hr, top, bot, wt, stem_bias[None, :], token_gain[None, :], wk, wvt, qz)

    def swap(x, flips0, flips1):
        pairs = []
        for a in range(nlat):
            for b in range(nlon):
                to = {"lat": a, "lon": b}
                for axis, bit in flips1 if b & 1 else flips0:
                    to[axis] ^= bit
                pairs.append((a * nlon + b, to["lat"] * nlon + to["lon"]))
        return lax.ppermute(x, ("lat", "lon"), pairs)

    def subsets(bits):
        return [[bit for n, bit in enumerate(bits) if m >> n & 1] for m in range(1, 1 << len(bits))]

    cores = [("lon", 1)]
    first, second = ("lon", 2), ("lat", 1)
    near = list(zip(subsets([second, first]), subsets([first, second])))
    far = [("lat", 1 << n) for n in range(1, nlat.bit_length() - 1)]
    far += [("lon", 1 << n) for n in range(2, nlon.bit_length() - 1)]
    groups = [far[n : n + 2] for n in range(0, len(far), 2)]

    one = shape((1, HR, lat), bf16)
    own, *others = call(fold_kernel, [one] * (HEADS // 2), 2)(keep, swap(send, cores, cores))
    states = [own] + [swap(x, *flips) for x, flips in zip(others, near)]
    own = call(functools.partial(group_kernel, last=False), one, 4)(*states)
    for n, bits in enumerate(groups):
        last = n == len(groups) - 1
        states = [own] + [swap(own, flips, flips) for flips in subsets(bits)]
        out = shape((1, HD, lat), bf16) if last else one
        own = call(functools.partial(group_kernel, last=last), out, len(states))(*states)
    parts = [own] + [swap(own, *flips) for flips in near]
    parts += [swap(x, cores, cores) for x in parts]
    latent_out = call(
        out_kernel, shape((lat, width), f32), HEADS + 2, smem=1, scratch=[VMEM((width, lat), f32)]
    )(place, *parts, out_weight, out_gain[None, :])
    return (tok, latent_out)


def solution(mesh):
    return jax.shard_map(
        shards,
        mesh=mesh,
        in_specs=(P(None, "lat", "lon"), P(), P(), P(), P(), P(), P(), P(), P(), P(), P()),
        out_specs=(P("lat", "lon", None), P()),
        check_vma=False,
    )
```

```python
import functools

import jax
import jax.numpy as jnp
from jax import lax
from jax.experimental import pallas as pl
from jax.experimental.pallas import tpu as pltpu
from jax.sharding import PartitionSpec as P

HEADS = 8
HD = 64
CP = 80
HR = 80
CT = 1024
VMEM = pltpu.VMEM
bf16 = jnp.bfloat16
f32 = jnp.float32
LOG2E = 1.4426950408889634


def call(kernel, out, n_in, scratch=(), smem=0, out_spaces=None):
    outs = out if isinstance(out, (list, tuple)) else [out]
    spaces = out_spaces or [VMEM] * len(outs)
    specs = [pl.BlockSpec(memory_space=s) for s in spaces]
    return pl.pallas_call(
        kernel,
        out_shape=out,
        in_specs=[pl.BlockSpec(memory_space=pltpu.SMEM)] * smem
        + [pl.BlockSpec(memory_space=VMEM)] * n_in,
        out_specs=specs if isinstance(out, (list, tuple)) else specs[0],
        scratch_shapes=list(scratch),
        compiler_params=pltpu.CompilerParams(vmem_limit_bytes=60 << 20),
    )


def shape(dims, dtype):
    return jax.ShapeDtypeStruct(tuple(dims), dtype)


def rows_norm(x, axis):
    mean = jnp.mean(x, axis=axis, keepdims=True)
    centred = x - mean
    spread = jnp.mean(centred * centred, axis=axis, keepdims=True)
    return centred * lax.rsqrt(spread + 1e-05)


def split3(x):
    hi = x.astype(bf16)
    rest = x - hi.astype(f32)
    mid = rest.astype(bf16)
    lo = (rest - mid.astype(f32)).astype(bf16)
    return hi, mid, lo


def weights_kernel(w_ref, kv_ref, wt_ref, wvt_ref, pad_ref):
    chan = w_ref.shape[0] // 16
    width = w_ref.shape[1]
    for k in range(16):
        pad_ref[(k + 1) * CP - 16 : (k + 1) * CP] = jnp.zeros((16, width), f32)
        pad_ref[k * CP : k * CP + chan] = w_ref[k * chan : (k + 1) * chan].astype(f32)
    for k in range(0, 16 * CP, 256):
        wt_ref[:, k : k + 256] = jnp.transpose(pad_ref[k : k + 256].astype(bf16))
    wvt_ref[...] = jnp.transpose(kv_ref[:, width:])


def query_kernel(gain_ref, latents_ref, lgain_ref, qw_ref, qz_ref):
    normed = (rows_norm(latents_ref[...], 1) * lgain_ref[...]).astype(bf16)
    query = jnp.dot(normed, qw_ref[...], preferred_element_type=f32).astype(bf16)
    qt = jnp.transpose(query.astype(f32))
    zero = jnp.zeros((HD, qt.shape[1]), bf16)
    for h in range(HEADS):
        scaled = qt[h * HD : (h + 1) * HD] * (gain_ref[h] * (LOG2E / HD**0.5))
        hi = scaled.astype(bf16)
        lo = (scaled - hi.astype(f32)).astype(bf16)
        parts = [hi, zero, lo, zero] if h % 2 == 0 else [zero, hi, zero, lo]
        for j, part in enumerate(parts):
            qz_ref[h, j * HD : (j + 1) * HD, :] = part


def places():
    lon, lat = lax.axis_index("lon"), lax.axis_index("lat")
    core, by, bx = lon & 1, (lon >> 1) & 1, lat & 1
    yx, xy = 2 * by + bx, 2 * bx + by
    return 4 * core + yx + core * (xy - yx), 4 * (1 - core) + xy + core * (yx - xy)


def encode_kernel(
    x_ref, hl_ref, hr_ref, top_ref, bot_ref, wt_ref, bias_ref, gain_ref, kv_ref, wvt_ref, qz_ref,
    tok_out, keep_ref, send_ref,
    y_ref, xs_ref, st_ref, tok_ref, k_ref, vt_ref, s_ref, col_ref, state_ref, peak_ref, side_ref, sems,
):
    chan, rows, cols = x_ref.shape
    half = cols // 2
    trows = rows // 2
    width = kv_ref.shape[0]
    tokens = trows * half
    lat = qz_ref.shape[2]

    i = lax.broadcasted_iota(jnp.int32, (256, 256), 0)
    j = lax.broadcasted_iota(jnp.int32, (256, 256), 1)
    perm = jnp.where(((i >> 4) == (j & 15)) & ((i & 15) == (j >> 4)), 1.0, 0.0).astype(bf16)
    for g in range(CP // 16):
        n = min(16, chan - 16 * g)
        for b in range(rows // 16):
            x = x_ref[16 * g : 16 * g + n, 16 * b : 16 * b + 16, :].reshape(n * 16, cols)
            y = jnp.dot(perm[:, : n * 16], x, preferred_element_type=f32).astype(bf16)
            y_ref[1 + 16 * b : 17 + 16 * b, 16 * g : 16 * g + 16, :] = y.reshape(16, 16, cols)
    y_ref[0] = top_ref[:CP]
    y_ref[rows + 1] = bot_ref[:CP]

    ci = lax.broadcasted_iota(jnp.int32, (cols, cols), 0)
    cj = lax.broadcasted_iota(jnp.int32, (cols, cols), 1)
    want = jnp.where(cj < half, 2 * cj, 2 * (cj - half) + 1)
    select = jnp.where(ci == want, 1.0, 0.0).astype(bf16)
    lane = lax.broadcasted_iota(jnp.int32, (CP, half), 1)
    side_ref[...] = jnp.zeros(side_ref.shape, f32)
    for n, ref in enumerate((hl_ref, hr_ref)):
        side_ref[n, 1 : rows + 1] = ref[...].astype(f32)
        for r, row in ((0, top_ref), (rows + 1, bot_ref)):
            side_ref[n, r : r + 1] = row[CP + 16 * n : CP + 16 * n + 16, :128].astype(f32)[:1]
    left_all, right_all = (jnp.transpose(side_ref[n])[:CP] for n in range(2))
    for p in range((rows + 2) // 2):
        pair = y_ref[2 * p : 2 * p + 2].reshape(2 * CP, cols)
        sel = jnp.dot(pair, select, preferred_element_type=f32)
        for q in range(2):
            r = 2 * p + q
            left, right = left_all[:, r : r + 1], right_all[:, r : r + 1]
            even = sel[q * CP : (q + 1) * CP, :half]
            odd = sel[q * CP : (q + 1) * CP, half:]
            first = jnp.where(lane == 0, left, pltpu.roll(odd, 1, 1))
            last = jnp.where(lane == half - 1, right, pltpu.roll(even, half - 1, 1))
            for kx, v in enumerate((first, even, odd, last)):
                xs_ref[r, kx * CP : (kx + 1) * CP, :] = v.astype(bf16)

    for h in range(HEADS):
        vt_ref[h * HR + HD : (h + 1) * HR, :] = jnp.ones((HR - HD, tokens), bf16)

    for n, row in enumerate((bias_ref, gain_ref)):
        col_ref[n] = jnp.transpose(jnp.broadcast_to(row[...], (128, width)))

    def column(n):
        return jnp.concatenate([col_ref[n]] * (half // 128), axis=1)

    def stem(r, slot):
        patch = xs_ref[pl.ds(2 * r, 4)].reshape(16 * CP, half)
        st_ref[slot] = jnp.dot(wt_ref[...], patch, preferred_element_type=f32)

    def finish(r, slot):
        value = rows_norm(st_ref[slot] + column(0), 0) * column(1)
        tt = value.astype(bf16)
        tok = jnp.transpose(tt)
        tok_ref[r] = tok
        pltpu.make_async_copy(tok_ref.at[r], tok_out.at[r], sems.at[r]).start()
        at = pl.ds(pl.multiple_of(r * half, half), half)
        k_ref[at, :] = jnp.dot(tok, kv_ref[:, :width], preferred_element_type=f32).astype(bf16)
        vt = jnp.dot(wvt_ref[...], tt, preferred_element_type=f32).astype(bf16)
        for h in range(HEADS):
            vt_ref[h * HR : h * HR + HD, at] = vt[h * HD : (h + 1) * HD]

    stem(0, 0)

    def band(n, carry):
        r = 2 * n
        stem(r + 1, 1)
        finish(r, 0)
        stem(jnp.minimum(r + 2, trows - 1), 0)
        finish(r + 1, 1)
        return carry

    lax.fori_loop(0, trows // 2, band, 0)

    def produce(h, c, slot):
        pair = pl.ds(pl.multiple_of((h >> 1) * (2 * HD), 2 * HD), 2 * HD)
        keys = k_ref[c * CT : (c + 1) * CT, pair]
        keys = jnp.concatenate([keys, keys], axis=1)
        s = jnp.dot(keys, qz_ref[h], preferred_element_type=f32)
        s_ref[slot] = s
        return jnp.max(s, axis=0, keepdims=True)

    chunks = tokens // CT
    mine, other = places()

    def head_of(t):
        late = t >> (HEADS.bit_length() - 2)
        return (t & (HEADS // 2 - 1)) ^ (mine + late * (other - mine))

    def head(t, most):
        h = head_of(t)
        after = head_of(jnp.minimum(t + 1, HEADS - 1))
        peak = jnp.full((1, lat), -1e30, f32)
        state = jnp.zeros((HR, lat), f32)
        for c in range(chunks):
            if c + 1 < chunks:
                following = produce(h, c + 1, (c + 1) % 2)
            else:
                following = produce(after, 0, (c + 1) % 2)
            newpeak = jnp.maximum(peak, jnp.ceil(most))
            fold = jnp.exp2(peak - newpeak)
            weights = jnp.exp2(s_ref[c % 2] - newpeak).astype(bf16)
            values = vt_ref[pl.ds(pl.multiple_of(h * HR, 16), HR), c * CT : (c + 1) * CT]
            state = state * fold + jnp.dot(values, weights, preferred_element_type=f32)
            peak, most = newpeak, following
        state_ref[t] = state
        peak_ref[t] = peak
        return most

    lax.fori_loop(0, HEADS, head, produce(head_of(0), 0, 0))
    for t in range(HEADS):
        state = state_ref[t]
        packed = pack(state[:HD], state[HD : HD + 1], peak_ref[t])
        (keep_ref if t < HEADS // 2 else send_ref)[t % (HEADS // 2)] = packed
    for r in range(trows):
        pltpu.make_async_copy(tok_ref.at[r], tok_out.at[r], sems.at[r]).wait()


def encode_scratch(rows, cols, width, lat):
    half, trows = cols // 2, rows // 2
    tokens = trows * half
    return [
        VMEM((rows + 2, CP, cols), bf16),
        VMEM((rows + 2, 4 * CP, half), bf16),
        VMEM((2, width, half), f32),
        VMEM((trows, half, width), bf16),
        VMEM((tokens, width), bf16),
        VMEM((HEADS * HR, tokens), bf16),
        VMEM((2, CT, lat), f32),
        VMEM((2, width, 128), f32),
        VMEM((HEADS, HR, lat), f32),
        VMEM((HEADS, 1, lat), f32),
        VMEM((2, 128, 128), f32),
        pltpu.SemaphoreType.DMA((trows,)),
    ]


def pack(sums, total, peak):
    lat = sums.shape[1]
    row = lax.broadcasted_iota(jnp.int32, (16, lat), 0)
    tail = jnp.zeros((16, lat), f32)
    for n, part in enumerate(split3(total) + split3(peak)):
        tail = jnp.where(row == n, part.astype(f32), tail)
    return jnp.concatenate([sums.astype(bf16), tail.astype(bf16)], axis=0)


def unpack(state):
    tail = state[HD:].astype(f32)
    total = (tail[0:1] + tail[1:2]) + tail[2:3]
    peak = (tail[3:4] + tail[4:5]) + tail[5:6]
    return state[:HD].astype(f32), total, peak


def combined(a, b):
    sums_a, total_a, peak_a = a
    sums_b, total_b, peak_b = b
    peak = jnp.maximum(peak_a, peak_b)
    fold_a = jnp.exp2(peak_a - peak)
    fold_b = jnp.exp2(peak_b - peak)
    return sums_a * fold_a + sums_b * fold_b, total_a * fold_a + total_b * fold_b, peak


def open_state(state):
    tail = state[:, HD:].astype(f32)
    total = (tail[:, 0:1] + tail[:, 1:2]) + tail[:, 2:3]
    peak = (tail[:, 3:4] + tail[:, 4:5]) + tail[:, 5:6]
    return state[:, :HD].astype(f32), total, peak


def rounded(x):
    return lax.reduce_precision(x, 8, 7)


def closed_state(sums, total, peak):
    parts = [sums]
    for x in (total, peak):
        hi = rounded(x)
        mid = rounded(x - hi)
        parts += [hi, mid, rounded((x - hi) - mid)]
    parts.append(jnp.zeros((sums.shape[0], HR - HD - 6, sums.shape[2]), f32))
    return jnp.concatenate(parts, 1).astype(bf16)


def merged(states):
    states = [open_state(x) for x in states]
    while len(states) > 1:
        states = [combined(*states[n : n + 2]) for n in range(0, len(states), 2)]
    return states[0]


def out_kernel(*refs):
    parts, (wo_ref, gain_ref, out_ref, all_ref) = refs[:HEADS], refs[HEADS:]
    half, place = HEADS // 2, places()
    for t in range(HEADS):
        value = parts[t][0]
        h = (t % half) ^ place[t // half]
        all_ref[pl.ds(pl.multiple_of(h * HD, HD), HD), :] = value.astype(f32)
    attended = jnp.transpose(all_ref[...]).astype(bf16)
    mixed = jnp.dot(attended, wo_ref[...], preferred_element_type=f32)
    out_ref[...] = rows_norm(mixed, 1) * gain_ref[...]


def shards(
    field, stem_weight, stem_bias, token_gain, kv_weight, latents,
    latent_gain, query_weight, head_gain, out_weight, out_gain,
):
    chan, rows, cols = field.shape
    width = stem_weight.shape[1]
    lat = latents.shape[0]
    nlat = lax.axis_size("lat")
    nlon = lax.axis_size("lon")
    half = cols // 2
    trows = rows // 2

    ahead = [(i, (i + 1) % nlon) for i in range(nlon)]
    back = [(t, s) for s, t in ahead]

    def side(c):
        return jnp.pad(field[:, :, c].T, ((0, 0), (0, 128 - chan)))

    hl = lax.ppermute(side(cols - 1), "lon", ahead)
    hr = lax.ppermute(side(0), "lon", back)
    wt, wvt = call(
        weights_kernel,
        [shape((width, 16 * CP), bf16), shape((width, width), bf16)],
        2,
        scratch=[VMEM((16 * CP, width), f32)],
    )(stem_weight, kv_weight)
    hl, hr, wt, wvt = lax.optimization_barrier((hl, hr, wt, wvt))

    def edge(r):
        corners = [jnp.pad(h[r : r + 1], ((0, 15), (0, cols - 128))) for h in (hl, hr)]
        return jnp.concatenate([jnp.pad(field[:, r, :], ((0, CP - chan), (0, 0)))] + corners)

    low, high = edge(rows - 1), edge(0)
    low, high, latents = lax.optimization_barrier((low, high, latents))
    up = [(i, i + 1) for i in range(nlat - 1)]
    down = [(t, s) for s, t in up]
    top = lax.ppermute(low, "lat", up)
    bot = lax.ppermute(high, "lat", down)
    qz = call(query_kernel, shape((HEADS, 4 * HD, lat), bf16), 3, smem=1)(
        head_gain, latents, latent_gain[None, :], query_weight
    )

    state = shape((HEADS // 2, HR, lat), bf16)
    tok, keep, send = call(
        encode_kernel,
        [shape((trows, half, width), bf16), state, state],
        11,
        out_spaces=[pl.ANY, VMEM, VMEM],
        scratch=encode_scratch(rows, cols, width, lat),
    )(field, hl, hr, top, bot, wt, stem_bias[None, :], token_gain[None, :], kv_weight, wvt, qz)

    def swap(x, flips0, flips1):
        pairs = []
        for a in range(nlat):
            for b in range(nlon):
                to = {"lat": a, "lon": b}
                for axis, bit in flips1 if b & 1 else flips0:
                    to[axis] ^= bit
                pairs.append((a * nlon + b, to["lat"] * nlon + to["lon"]))
        return lax.ppermute(x, ("lat", "lon"), pairs)

    def subsets(bits):
        return [[bit for n, bit in enumerate(bits) if m >> n & 1] for m in range(1, 1 << len(bits))]

    cores = [("lon", 1)]
    first, second = ("lon", 2), ("lat", 1)
    near = list(zip(subsets([second, first]), subsets([first, second])))
    far = [("lat", 1 << n) for n in range(1, nlat.bit_length() - 1)]
    far += [("lon", 1 << n) for n in range(2, nlon.bit_length() - 1)]
    groups = [far[n : n + 2] for n in range(0, len(far), 2)]

    four = closed_state(*merged([keep, swap(send, cores, cores)]))
    own, *others = (four[n : n + 1] for n in range(HEADS // 2))
    states = [own] + [swap(x, *flips) for x, flips in zip(others, near)]
    for bits in groups:
        own = closed_state(*merged(states))
        states = [own] + [swap(own, flips, flips) for flips in subsets(bits)]
    sums, total, _ = merged(states)
    own = (sums / total).astype(bf16)
    parts = [own] + [swap(own, *flips) for flips in near]
    parts += [swap(x, cores, cores) for x in parts]
    latent_out = call(
        out_kernel, shape((lat, width), f32), HEADS + 2, scratch=[VMEM((width, lat), f32)]
    )(*parts, out_weight, out_gain[None, :])
    return (tok, latent_out)


def solution(mesh):
    return jax.shard_map(
        shards,
        mesh=mesh,
        in_specs=(P(None, "lat", "lon"), P(), P(), P(), P(), P(), P(), P(), P(), P(), P()),
        out_specs=(P("lat", "lon", None), P()),
        check_vma=False,
    )
```

```python
import functools

import jax
import jax.numpy as jnp
from jax import lax
from jax.experimental import pallas as pl
from jax.experimental.pallas import tpu as pltpu
from jax.sharding import PartitionSpec as P

HEADS = 8
HD = 64
CP = 80
HR = 80
CT = 1024
VMEM = pltpu.VMEM
bf16 = jnp.bfloat16
f32 = jnp.float32
LIMIT = 44 << 20
LOG2E = 1.4426950408889634


def call(kernel, out, n_in, scratch=(), smem=0, out_spaces=None, aliases=None):
    outs = out if isinstance(out, (list, tuple)) else [out]
    spaces = out_spaces or [VMEM] * len(outs)
    specs = [pl.BlockSpec(memory_space=s) for s in spaces]
    kept = [VMEM(o.shape, o.dtype) if s is VMEM else o for o, s in zip(outs, spaces)]
    single = not isinstance(out, (list, tuple))
    fn = pl.pallas_call(
        kernel,
        out_shape=kept[0] if single else kept,
        in_specs=[pl.BlockSpec(memory_space=pltpu.SMEM)] * smem
        + [pl.BlockSpec(memory_space=VMEM)] * n_in,
        out_specs=specs[0] if single else specs,
        scratch_shapes=list(scratch),
        input_output_aliases=aliases or {},
        compiler_params=pltpu.CompilerParams(vmem_limit_bytes=LIMIT),
    )

    def run(*args):
        held = [pltpu.with_memory_space_constraint(x, VMEM) for x in args[smem:]]
        return fn(*args[:smem], *held)

    return run


def shape(dims, dtype):
    return jax.ShapeDtypeStruct(tuple(dims), dtype)


def rows_norm(x, axis):
    mean = jnp.mean(x, axis=axis, keepdims=True)
    centred = x - mean
    spread = jnp.mean(centred * centred, axis=axis, keepdims=True)
    return centred * lax.rsqrt(spread + 1e-05)


def split3(x):
    hi = x.astype(bf16)
    rest = x - hi.astype(f32)
    mid = rest.astype(bf16)
    lo = (rest - mid.astype(f32)).astype(bf16)
    return hi, mid, lo


def weights_kernel(w_ref, kv_ref, wt_ref, wvt_ref, pad_ref):
    chan = w_ref.shape[0] // 16
    width = w_ref.shape[1]
    for k in range(16):
        pad_ref[(k + 1) * CP - 16 : (k + 1) * CP] = jnp.zeros((16, width), f32)
        pad_ref[k * CP : k * CP + chan] = w_ref[k * chan : (k + 1) * chan].astype(f32)
    for k in range(0, 16 * CP, 256):
        wt_ref[:, k : k + 256] = jnp.transpose(pad_ref[k : k + 256].astype(bf16))
    wvt_ref[...] = jnp.transpose(kv_ref[:, width:])


def query_kernel(gain_ref, latents_ref, lgain_ref, qw_ref, qz_ref):
    normed = (rows_norm(latents_ref[...], 1) * lgain_ref[...]).astype(bf16)
    query = jnp.dot(normed, qw_ref[...], preferred_element_type=f32).astype(bf16)
    qt = jnp.transpose(query.astype(f32))
    zero = jnp.zeros((HD, qt.shape[1]), bf16)
    for h in range(HEADS):
        scaled = qt[h * HD : (h + 1) * HD] * (gain_ref[h] * (LOG2E / HD**0.5))
        hi = scaled.astype(bf16)
        lo = (scaled - hi.astype(f32)).astype(bf16)
        parts = [hi, zero, lo, zero] if h % 2 == 0 else [zero, hi, zero, lo]
        for j, part in enumerate(parts):
            qz_ref[h, j * HD : (j + 1) * HD, :] = part


def places():
    lon, lat = lax.axis_index("lon"), lax.axis_index("lat")
    core, by, bx = lon & 1, (lon >> 1) & 1, lat & 1
    yx, xy = 2 * by + bx, 2 * bx + by
    return 4 * core + yx + core * (xy - yx), 4 * (1 - core) + xy + core * (yx - xy)


def edges_kernel(x_ref, first_ref, last_ref, low_ref, high_ref, row_ref):
    chan, rows, cols = x_ref.shape
    lane = lax.broadcasted_iota(jnp.int32, (rows, 128), 1)
    first = jnp.zeros((rows, 128), f32)
    last = jnp.zeros((rows, 128), f32)
    row_ref[...] = jnp.zeros(row_ref.shape, f32)
    for ch in range(chan):
        first = jnp.where(lane == ch, x_ref[ch, :, :128].astype(f32)[:, :1], first)
        last = jnp.where(lane == ch, x_ref[ch, :, cols - 128 :].astype(f32)[:, 127:], last)
        row_ref[0, ch : ch + 1, :] = x_ref[ch, :16, :].astype(f32)[:1]
        row_ref[1, ch : ch + 1, :] = x_ref[ch, rows - 16 :, :].astype(f32)[15:]
    first_ref[...] = first.astype(bf16)
    last_ref[...] = last.astype(bf16)
    low_ref[...] = row_ref[0].astype(bf16)
    high_ref[...] = row_ref[1].astype(bf16)


def selection(cols):
    ci = lax.broadcasted_iota(jnp.int32, (cols, cols), 0)
    cj = lax.broadcasted_iota(jnp.int32, (cols, cols), 1)
    want = jnp.where(cj < cols // 2, 2 * cj, 2 * (cj - cols // 2) + 1)
    return jnp.where(ci == want, 1.0, 0.0).astype(bf16)


def spread(pair, select, xs_ref, where, sides):
    half = select.shape[0] // 2
    lane = lax.broadcasted_iota(jnp.int32, (CP, half), 1)
    sel = jnp.dot(pair, select, preferred_element_type=f32)
    for q, (left, right) in enumerate(sides):
        even = sel[q * CP : (q + 1) * CP, :half]
        odd = sel[q * CP : (q + 1) * CP, half:]
        first = jnp.where(lane == 0, left, pltpu.roll(odd, 1, 1))
        last = jnp.where(lane == half - 1, right, pltpu.roll(even, half - 1, 1))
        for kx, v in enumerate((first, even, odd, last)):
            xs_ref[where[q], kx * CP : (kx + 1) * CP, :] = v.astype(bf16)


def turned(ref, side_ref):
    side_ref[...] = jnp.zeros(side_ref.shape, f32)
    side_ref[: ref.shape[0]] = ref[...].astype(f32)
    return jnp.transpose(side_ref[...])[:CP]


def select_kernel(x_ref, hl_ref, hr_ref, xs_ref, y_ref, side_ref):
    chan, rows, cols = x_ref.shape

    i = lax.broadcasted_iota(jnp.int32, (256, 256), 0)
    j = lax.broadcasted_iota(jnp.int32, (256, 256), 1)
    perm = jnp.where(((i >> 4) == (j & 15)) & ((i & 15) == (j >> 4)), 1.0, 0.0).astype(bf16)
    for b in range(rows // 16):
        for g in range(CP // 16):
            n = min(16, chan - 16 * g)
            x = x_ref[16 * g : 16 * g + n, 16 * b : 16 * b + 16, :].reshape(n * 16, cols)
            y = jnp.dot(perm[:, : n * 16], x, preferred_element_type=f32).astype(bf16)
            y_ref[16 * b : 16 * b + 16, 16 * g : 16 * g + 16, :] = y.reshape(16, 16, cols)

    select = selection(cols)
    left, right = turned(hl_ref, side_ref.at[0]), turned(hr_ref, side_ref.at[1])
    for r in range(0, rows, 2):
        pair = y_ref[r : r + 2].reshape(2 * CP, cols)
        sides = [(left[:, q : q + 1], right[:, q : q + 1]) for q in (r, r + 1)]
        spread(pair, select, xs_ref, (r + 1, r + 2), sides)


def encode_kernel(
    xs_in, top_ref, bot_ref, wt_ref, bias_ref, gain_ref, kv_ref, wvt_ref, qz_ref,
    tok_out, keep_ref, send_ref, xs_ref,
    st_ref, tok_ref, k_ref, vt_ref, s_ref, col_ref, state_ref, peak_ref, side_ref, sems,
):
    trows, half, width = tok_ref.shape
    rows, cols = 2 * trows, 2 * half
    tokens = trows * half
    lat = qz_ref.shape[2]

    pair = jnp.concatenate([top_ref[:CP], bot_ref[:CP]])
    sides = []
    for n, ref in enumerate((top_ref, bot_ref)):
        corners = turned(ref.at[CP:, :128], side_ref.at[n])
        sides.append((corners[:, 0:1], corners[:, 16:17]))
    spread(pair, selection(cols), xs_ref, (0, rows + 1), sides)

    for h in range(HEADS):
        vt_ref[h * HR + HD : (h + 1) * HR, :] = jnp.ones((HR - HD, tokens), bf16)

    for n, row in enumerate((bias_ref, gain_ref)):
        col_ref[n] = jnp.transpose(jnp.broadcast_to(row[...], (128, width)))

    def column(n):
        return jnp.concatenate([col_ref[n]] * (half // 128), axis=1)

    def stem(r, slot):
        patch = xs_ref[pl.ds(2 * r, 4)].reshape(16 * CP, half)
        st_ref[slot] = jnp.dot(wt_ref[...], patch, preferred_element_type=f32)

    def finish(r, slot):
        value = rows_norm(st_ref[slot] + column(0), 0) * column(1)
        tt = value.astype(bf16)
        tok = jnp.transpose(tt)
        tok_ref[r] = tok
        pltpu.make_async_copy(tok_ref.at[r], tok_out.at[r], sems.at[r]).start()
        at = pl.ds(pl.multiple_of(r * half, half), half)
        k_ref[at, :] = jnp.dot(tok, kv_ref[:, :width], preferred_element_type=f32).astype(bf16)
        vt = jnp.dot(wvt_ref[...], tt, preferred_element_type=f32).astype(bf16)
        for h in range(HEADS):
            vt_ref[h * HR : h * HR + HD, at] = vt[h * HD : (h + 1) * HD]

    stem(0, 0)

    def band(n, carry):
        r = 2 * n
        stem(r + 1, 1)
        finish(r, 0)
        stem(jnp.minimum(r + 2, trows - 1), 0)
        finish(r + 1, 1)
        return carry

    lax.fori_loop(0, trows // 2, band, 0)

    def produce(h, c, slot):
        pair = pl.ds(pl.multiple_of((h >> 1) * (2 * HD), 2 * HD), 2 * HD)
        keys = k_ref[c * CT : (c + 1) * CT, pair]
        keys = jnp.concatenate([keys, keys], axis=1)
        s = jnp.dot(keys, qz_ref[h], preferred_element_type=f32)
        s_ref[slot] = s
        return jnp.max(s, axis=0, keepdims=True)

    chunks = tokens // CT
    mine, other = places()

    def head_of(t):
        late = t >> (HEADS.bit_length() - 2)
        return (t & (HEADS // 2 - 1)) ^ (mine + late * (other - mine))

    def head(t, most):
        h = head_of(t)
        after = head_of(jnp.minimum(t + 1, HEADS - 1))
        peak = jnp.full((1, lat), -1e30, f32)
        state = jnp.zeros((HR, lat), f32)
        for c in range(chunks):
            if c + 1 < chunks:
                following = produce(h, c + 1, (c + 1) % 2)
            else:
                following = produce(after, 0, (c + 1) % 2)
            newpeak = jnp.maximum(peak, jnp.ceil(most))
            fold = jnp.exp2(peak - newpeak)
            weights = jnp.exp2(s_ref[c % 2] - newpeak).astype(bf16)
            values = vt_ref[pl.ds(pl.multiple_of(h * HR, 16), HR), c * CT : (c + 1) * CT]
            state = state * fold + jnp.dot(values, weights, preferred_element_type=f32)
            peak, most = newpeak, following
        state_ref[t] = state
        peak_ref[t] = peak
        return most

    lax.fori_loop(0, HEADS, head, produce(head_of(0), 0, 0))
    for t in range(HEADS):
        state = state_ref[t]
        packed = pack(state[:HD], state[HD : HD + 1], peak_ref[t])
        (keep_ref if t < HEADS // 2 else send_ref)[t % (HEADS // 2)] = packed
    for r in range(trows):
        pltpu.make_async_copy(tok_ref.at[r], tok_out.at[r], sems.at[r]).wait()


def encode_scratch(rows, cols, width, lat):
    half, trows = cols // 2, rows // 2
    tokens = trows * half
    return [
        VMEM((2, width, half), f32),
        VMEM((trows, half, width), bf16),
        VMEM((tokens, width), bf16),
        VMEM((HEADS * HR, tokens), bf16),
        VMEM((2, CT, lat), f32),
        VMEM((2, width, 128), f32),
        VMEM((HEADS, HR, lat), f32),
        VMEM((HEADS, 1, lat), f32),
        VMEM((2, 128, 128), f32),
        pltpu.SemaphoreType.DMA((trows,)),
    ]


def pack(sums, total, peak):
    lat = sums.shape[1]
    row = lax.broadcasted_iota(jnp.int32, (16, lat), 0)
    tail = jnp.zeros((16, lat), f32)
    for n, part in enumerate(split3(total) + split3(peak)):
        tail = jnp.where(row == n, part.astype(f32), tail)
    return jnp.concatenate([sums.astype(bf16), tail.astype(bf16)], axis=0)


def unpack(state):
    tail = state[HD:].astype(f32)
    total = (tail[0:1] + tail[1:2]) + tail[2:3]
    peak = (tail[3:4] + tail[4:5]) + tail[5:6]
    return state[:HD].astype(f32), total, peak


def combined(a, b):
    sums_a, total_a, peak_a = a
    sums_b, total_b, peak_b = b
    peak = jnp.maximum(peak_a, peak_b)
    fold_a = jnp.exp2(peak_a - peak)
    fold_b = jnp.exp2(peak_b - peak)
    return sums_a * fold_a + sums_b * fold_b, total_a * fold_a + total_b * fold_b, peak


def open_state(state):
    tail = state[:, HD:].astype(f32)
    total = (tail[:, 0:1] + tail[:, 1:2]) + tail[:, 2:3]
    peak = (tail[:, 3:4] + tail[:, 4:5]) + tail[:, 5:6]
    return state[:, :HD].astype(f32), total, peak


def rounded(x):
    return lax.reduce_precision(x, 8, 7)


def closed_state(sums, total, peak):
    parts = [sums]
    for x in (total, peak):
        hi = rounded(x)
        mid = rounded(x - hi)
        parts += [hi, mid, rounded((x - hi) - mid)]
    parts.append(jnp.zeros((sums.shape[0], HR - HD - 6, sums.shape[2]), f32))
    return jnp.concatenate(parts, 1).astype(bf16)


def merged(states):
    states = [open_state(x) for x in states]
    while len(states) > 1:
        states = [combined(*states[n : n + 2]) for n in range(0, len(states), 2)]
    return states[0]


def out_kernel(*refs):
    parts, (wo_ref, gain_ref, out_ref, all_ref) = refs[:HEADS], refs[HEADS:]
    half, place = HEADS // 2, places()
    for t in range(HEADS):
        value = parts[t][0]
        h = (t % half) ^ place[t // half]
        all_ref[pl.ds(pl.multiple_of(h * HD, HD), HD), :] = value.astype(f32)
    attended = jnp.transpose(all_ref[...]).astype(bf16)
    mixed = jnp.dot(attended, wo_ref[...], preferred_element_type=f32)
    out_ref[...] = rows_norm(mixed, 1) * gain_ref[...]


def shards(
    field, stem_weight, stem_bias, token_gain, kv_weight, latents,
    latent_gain, query_weight, head_gain, out_weight, out_gain,
):
    chan, rows, cols = field.shape
    width = stem_weight.shape[1]
    lat = latents.shape[0]
    nlat = lax.axis_size("lat")
    nlon = lax.axis_size("lon")
    half = cols // 2
    trows = rows // 2

    ahead = [(i, (i + 1) % nlon) for i in range(nlon)]
    back = [(t, s) for s, t in ahead]

    edge = shape((rows, 128), bf16)
    line = shape((CP, cols), bf16)
    first, last, low, high = call(
        edges_kernel, [edge, edge, line, line], 1, scratch=[VMEM((2, CP, cols), f32)]
    )(field)
    hl = lax.ppermute(last, "lon", ahead)
    hr = lax.ppermute(first, "lon", back)
    wt, wvt = call(
        weights_kernel,
        [shape((width, 16 * CP), bf16), shape((width, width), bf16)],
        2,
        scratch=[VMEM((16 * CP, width), f32)],
    )(stem_weight, kv_weight)
    hl, hr, wt, wvt = lax.optimization_barrier((hl, hr, wt, wvt))

    def framed(line, r):
        corners = [jnp.pad(h[r : r + 1], ((0, 15), (0, cols - 128))) for h in (hl, hr)]
        return jnp.concatenate([line] + corners)

    low, high = framed(low, 0), framed(high, rows - 1)
    low, high, latents, hl = lax.optimization_barrier((low, high, latents, hl))
    up = [(i, i + 1) for i in range(nlat - 1)]
    down = [(t, s) for s, t in up]
    top = lax.ppermute(high, "lat", up)
    bot = lax.ppermute(low, "lat", down)
    qz = call(query_kernel, shape((HEADS, 4 * HD, lat), bf16), 3, smem=1)(
        head_gain, latents, latent_gain[None, :], query_weight
    )

    patches = shape((rows + 2, 4 * CP, half), bf16)
    xs = call(
        select_kernel,
        patches,
        3,
        scratch=[VMEM((rows, CP, cols), bf16), VMEM((2, 128, 128), f32)],
    )(field, hl, hr)
    state = shape((HEADS // 2, HR, lat), bf16)
    tok, keep, send, _ = call(
        encode_kernel,
        [shape((trows, half, width), bf16), state, state, patches],
        9,
        out_spaces=[pl.ANY, VMEM, VMEM, VMEM],
        aliases={0: 3},
        scratch=encode_scratch(rows, cols, width, lat),
    )(xs, top, bot, wt, stem_bias[None, :], token_gain[None, :], kv_weight, wvt, qz)

    def swap(x, flips0, flips1):
        pairs = []
        for a in range(nlat):
            for b in range(nlon):
                to = {"lat": a, "lon": b}
                for axis, bit in flips1 if b & 1 else flips0:
                    to[axis] ^= bit
                pairs.append((a * nlon + b, to["lat"] * nlon + to["lon"]))
        return lax.ppermute(x, ("lat", "lon"), pairs)

    def subsets(bits):
        return [[bit for n, bit in enumerate(bits) if m >> n & 1] for m in range(1, 1 << len(bits))]

    cores = [("lon", 1)]
    first, second = ("lon", 2), ("lat", 1)
    near = list(zip(subsets([second, first]), subsets([first, second])))
    far = [("lat", 1 << n) for n in range(1, nlat.bit_length() - 1)]
    far += [("lon", 1 << n) for n in range(2, nlon.bit_length() - 1)]
    groups = [far[n : n + 2] for n in range(0, len(far), 2)]

    four = closed_state(*merged([keep, swap(send, cores, cores)]))
    own, *others = (four[n : n + 1] for n in range(HEADS // 2))
    states = [own] + [swap(x, *flips) for x, flips in zip(others, near)]
    for bits in groups:
        own = closed_state(*merged(states))
        states = [own] + [swap(own, flips, flips) for flips in subsets(bits)]
    sums, total, _ = merged(states)
    own = (sums / total).astype(bf16)
    parts = [own] + [swap(own, *flips) for flips in near]
    parts += [swap(x, cores, cores) for x in parts]
    latent_out = call(
        out_kernel, shape((lat, width), f32), HEADS + 2, scratch=[VMEM((width, lat), f32)]
    )(*parts, out_weight, out_gain[None, :])
    return (tok, latent_out)


def solution(mesh):
    return jax.shard_map(
        shards,
        mesh=mesh,
        in_specs=(P(None, "lat", "lon"), P(), P(), P(), P(), P(), P(), P(), P(), P(), P()),
        out_specs=(P("lat", "lon", None), P()),
        check_vma=False,
    )
```

```python
import functools

import jax
import jax.numpy as jnp
from jax import lax
from jax.experimental import pallas as pl
from jax.experimental.pallas import tpu as pltpu
from jax.sharding import PartitionSpec as P

HEADS = 8
HD = 64
CP = 80
HR = 80
CT = 1024
VMEM = pltpu.VMEM
bf16 = jnp.bfloat16
f32 = jnp.float32
LIMIT = 44 << 20
CORNER = CP - 8
LOG2E = 1.4426950408889634


def call(kernel, out, n_in, scratch=(), smem=0, out_spaces=None, aliases=None):
    outs = out if isinstance(out, (list, tuple)) else [out]
    spaces = out_spaces or [VMEM] * len(outs)
    specs = [pl.BlockSpec(memory_space=s) for s in spaces]
    kept = [VMEM(o.shape, o.dtype) if s is VMEM else o for o, s in zip(outs, spaces)]
    single = not isinstance(out, (list, tuple))
    fn = pl.pallas_call(
        kernel,
        out_shape=kept[0] if single else kept,
        in_specs=[pl.BlockSpec(memory_space=pltpu.SMEM)] * smem
        + [pl.BlockSpec(memory_space=VMEM)] * n_in,
        out_specs=specs[0] if single else specs,
        scratch_shapes=list(scratch),
        input_output_aliases=aliases or {},
        compiler_params=pltpu.CompilerParams(vmem_limit_bytes=LIMIT),
    )

    def run(*args):
        held = [pltpu.with_memory_space_constraint(x, VMEM) for x in args[smem:]]
        return fn(*args[:smem], *held)

    return run


def shape(dims, dtype):
    return jax.ShapeDtypeStruct(tuple(dims), dtype)


def rows_norm(x, axis):
    mean = jnp.mean(x, axis=axis, keepdims=True)
    centred = x - mean
    spread = jnp.mean(centred * centred, axis=axis, keepdims=True)
    return centred * lax.rsqrt(spread + 1e-05)


def split3(x):
    hi = x.astype(bf16)
    rest = x - hi.astype(f32)
    mid = rest.astype(bf16)
    lo = (rest - mid.astype(f32)).astype(bf16)
    return hi, mid, lo


def weights_kernel(w_ref, kv_ref, wt_ref, wvt_ref, pad_ref):
    chan = w_ref.shape[0] // 16
    width = w_ref.shape[1]
    for k in range(16):
        pad_ref[(k + 1) * CP - 16 : (k + 1) * CP] = jnp.zeros((16, width), f32)
        pad_ref[k * CP : k * CP + chan] = w_ref[k * chan : (k + 1) * chan].astype(f32)
    for k in range(0, 16 * CP, 256):
        wt_ref[:, k : k + 256] = jnp.transpose(pad_ref[k : k + 256].astype(bf16))
    wvt_ref[...] = jnp.transpose(kv_ref[:, width:])


def query_kernel(gain_ref, latents_ref, lgain_ref, qw_ref, qz_ref):
    normed = (rows_norm(latents_ref[...], 1) * lgain_ref[...]).astype(bf16)
    query = jnp.dot(normed, qw_ref[...], preferred_element_type=f32).astype(bf16)
    qt = jnp.transpose(query.astype(f32))
    zero = jnp.zeros((HD, qt.shape[1]), bf16)
    for h in range(HEADS):
        scaled = qt[h * HD : (h + 1) * HD] * (gain_ref[h] * (LOG2E / HD**0.5))
        hi = scaled.astype(bf16)
        lo = (scaled - hi.astype(f32)).astype(bf16)
        parts = [hi, zero, lo, zero] if h % 2 == 0 else [zero, hi, zero, lo]
        for j, part in enumerate(parts):
            qz_ref[h, j * HD : (j + 1) * HD, :] = part


def places():
    lon, lat = lax.axis_index("lon"), lax.axis_index("lat")
    core, by, bx = lon & 1, (lon >> 1) & 1, lat & 1
    yx, xy = 2 * by + bx, 2 * bx + by
    return 4 * core + yx + core * (xy - yx), 4 * (1 - core) + xy + core * (yx - xy)


def edges_kernel(x_ref, first_ref, last_ref, low_ref, high_ref, row_ref):
    chan, rows, cols = x_ref.shape
    lane = lax.broadcasted_iota(jnp.int32, (rows, 128), 1)
    first = jnp.zeros((rows, 128), f32)
    last = jnp.zeros((rows, 128), f32)
    row_ref[...] = jnp.zeros(row_ref.shape, f32)
    for ch in range(chan):
        first = jnp.where(lane == ch, x_ref[ch, :, :128].astype(f32)[:, :1], first)
        last = jnp.where(lane == ch, x_ref[ch, :, cols - 128 :].astype(f32)[:, 127:], last)
        row_ref[0, ch : ch + 1, :] = x_ref[ch, :16, :].astype(f32)[:1]
        row_ref[1, ch : ch + 1, :] = x_ref[ch, rows - 16 :, :].astype(f32)[15:]
    first_ref[...] = first.astype(bf16)
    last_ref[...] = last.astype(bf16)
    low_ref[...] = row_ref[0].astype(bf16)
    high_ref[...] = row_ref[1].astype(bf16)


def selection(cols):
    ci = lax.broadcasted_iota(jnp.int32, (cols, cols), 0)
    cj = lax.broadcasted_iota(jnp.int32, (cols, cols), 1)
    want = jnp.where(cj < cols // 2, 2 * cj, 2 * (cj - cols // 2) + 1)
    return jnp.where(ci == want, 1.0, 0.0).astype(bf16)


def spread(pair, select, xs_ref, where, sides):
    half = select.shape[0] // 2
    lane = lax.broadcasted_iota(jnp.int32, (CP, half), 1)
    sel = jnp.dot(pair, select, preferred_element_type=f32)
    for q, (left, right) in enumerate(sides):
        even = sel[q * CP : (q + 1) * CP, :half]
        odd = sel[q * CP : (q + 1) * CP, half:]
        first = jnp.where(lane == 0, left, pltpu.roll(odd, 1, 1))
        last = jnp.where(lane == half - 1, right, pltpu.roll(even, half - 1, 1))
        for kx, v in enumerate((first, even, odd, last)):
            xs_ref[where[q], kx * CP : (kx + 1) * CP, :] = v.astype(bf16)


def turned(ref, side_ref):
    side_ref[...] = jnp.zeros(side_ref.shape, f32)
    side_ref[: ref.shape[0]] = ref[...].astype(f32)
    return jnp.transpose(side_ref[...])[:CP]


def select_kernel(x_ref, hl_ref, hr_ref, xs_ref, y_ref, side_ref):
    chan, rows, cols = x_ref.shape

    i = lax.broadcasted_iota(jnp.int32, (256, 256), 0)
    j = lax.broadcasted_iota(jnp.int32, (256, 256), 1)
    perm = jnp.where(((i >> 4) == (j & 15)) & ((i & 15) == (j >> 4)), 1.0, 0.0).astype(bf16)
    for b in range(rows // 16):
        for g in range(CP // 16):
            n = min(16, chan - 16 * g)
            x = x_ref[16 * g : 16 * g + n, 16 * b : 16 * b + 16, :].reshape(n * 16, cols)
            y = jnp.dot(perm[:, : n * 16], x, preferred_element_type=f32).astype(bf16)
            y_ref[16 * b : 16 * b + 16, 16 * g : 16 * g + 16, :] = y.reshape(16, 16, cols)

    select = selection(cols)
    left, right = turned(hl_ref, side_ref.at[0]), turned(hr_ref, side_ref.at[1])
    for r in range(0, rows, 2):
        pair = y_ref[r : r + 2].reshape(2 * CP, cols)
        sides = [(left[:, q : q + 1], right[:, q : q + 1]) for q in (r, r + 1)]
        spread(pair, select, xs_ref, (r + 1, r + 2), sides)


def encode_kernel(
    xs_in, top_ref, bot_ref, wt_ref, bias_ref, gain_ref, kv_ref, wvt_ref, qz_ref,
    tok_out, keep_ref, send_ref, xs_ref,
    st_ref, tok_ref, k_ref, vt_ref, s_ref, col_ref, state_ref, peak_ref, side_ref, sems,
):
    trows, half, width = tok_ref.shape
    rows, cols = 2 * trows, 2 * half
    tokens = trows * half
    lat = qz_ref.shape[2]

    pair = jnp.concatenate([top_ref[...], bot_ref[...]])
    sides = []
    for n, ref in enumerate((top_ref, bot_ref)):
        corners = turned(ref.at[CP - 16 :, :128], side_ref.at[n])
        at = CORNER - (CP - 16)
        sides.append((corners[:, at : at + 1], corners[:, at + 1 : at + 2]))
    spread(pair, selection(cols), xs_ref, (0, rows + 1), sides)

    for h in range(HEADS):
        vt_ref[h * HR + HD : (h + 1) * HR, :] = jnp.ones((HR - HD, tokens), bf16)

    for n, row in enumerate((bias_ref, gain_ref)):
        col_ref[n] = jnp.transpose(jnp.broadcast_to(row[...], (128, width)))

    def column(n):
        return jnp.concatenate([col_ref[n]] * (half // 128), axis=1)

    def stem(r, slot):
        patch = xs_ref[pl.ds(2 * r, 4)].reshape(16 * CP, half)
        st_ref[slot] = jnp.dot(wt_ref[...], patch, preferred_element_type=f32)

    def finish(r, slot):
        value = rows_norm(st_ref[slot] + column(0), 0) * column(1)
        tt = value.astype(bf16)
        tok = jnp.transpose(tt)
        tok_ref[r] = tok
        pltpu.make_async_copy(tok_ref.at[r], tok_out.at[r], sems.at[r]).start()
        at = pl.ds(pl.multiple_of(r * half, half), half)
        k_ref[at, :] = jnp.dot(tok, kv_ref[:, :width], preferred_element_type=f32).astype(bf16)
        vt = jnp.dot(wvt_ref[...], tt, preferred_element_type=f32).astype(bf16)
        for h in range(HEADS):
            vt_ref[h * HR : h * HR + HD, at] = vt[h * HD : (h + 1) * HD]

    stem(0, 0)

    def band(n, carry):
        r = 2 * n
        stem(r + 1, 1)
        finish(r, 0)
        stem(jnp.minimum(r + 2, trows - 1), 0)
        finish(r + 1, 1)
        return carry

    lax.fori_loop(0, trows // 2, band, 0)

    def produce(h, c, slot):
        pair = pl.ds(pl.multiple_of((h >> 1) * (2 * HD), 2 * HD), 2 * HD)
        keys = k_ref[c * CT : (c + 1) * CT, pair]
        keys = jnp.concatenate([keys, keys], axis=1)
        s = jnp.dot(keys, qz_ref[h], preferred_element_type=f32)
        s_ref[slot] = s
        return jnp.max(s, axis=0, keepdims=True)

    chunks = tokens // CT
    mine, other = places()

    def head_of(t):
        late = t >> (HEADS.bit_length() - 2)
        return (t & (HEADS // 2 - 1)) ^ (mine + late * (other - mine))

    def head(t, most):
        h = head_of(t)
        after = head_of(jnp.minimum(t + 1, HEADS - 1))
        peak = jnp.full((1, lat), -1e30, f32)
        state = jnp.zeros((HR, lat), f32)
        for c in range(chunks):
            if c + 1 < chunks:
                following = produce(h, c + 1, (c + 1) % 2)
            else:
                following = produce(after, 0, (c + 1) % 2)
            newpeak = jnp.maximum(peak, jnp.ceil(most))
            fold = jnp.exp2(peak - newpeak)
            weights = jnp.exp2(s_ref[c % 2] - newpeak).astype(bf16)
            values = vt_ref[pl.ds(pl.multiple_of(h * HR, 16), HR), c * CT : (c + 1) * CT]
            state = state * fold + jnp.dot(values, weights, preferred_element_type=f32)
            peak, most = newpeak, following
        state_ref[t] = state
        peak_ref[t] = peak
        return most

    lax.fori_loop(0, HEADS, head, produce(head_of(0), 0, 0))
    for t in range(HEADS):
        state = state_ref[t]
        packed = pack(state[:HD], state[HD : HD + 1], peak_ref[t])
        (keep_ref if t < HEADS // 2 else send_ref)[t % (HEADS // 2)] = packed
    for r in range(trows):
        pltpu.make_async_copy(tok_ref.at[r], tok_out.at[r], sems.at[r]).wait()


def encode_scratch(rows, cols, width, lat):
    half, trows = cols // 2, rows // 2
    tokens = trows * half
    return [
        VMEM((2, width, half), f32),
        VMEM((trows, half, width), bf16),
        VMEM((tokens, width), bf16),
        VMEM((HEADS * HR, tokens), bf16),
        VMEM((2, CT, lat), f32),
        VMEM((2, width, 128), f32),
        VMEM((HEADS, HR, lat), f32),
        VMEM((HEADS, 1, lat), f32),
        VMEM((2, 128, 128), f32),
        pltpu.SemaphoreType.DMA((trows,)),
    ]


def pack(sums, total, peak):
    lat = sums.shape[1]
    row = lax.broadcasted_iota(jnp.int32, (16, lat), 0)
    tail = jnp.zeros((16, lat), f32)
    for n, part in enumerate(split3(total) + split3(peak)):
        tail = jnp.where(row == n, part.astype(f32), tail)
    return jnp.concatenate([sums.astype(bf16), tail.astype(bf16)], axis=0)


def unpack(state):
    tail = state[HD:].astype(f32)
    total = (tail[0:1] + tail[1:2]) + tail[2:3]
    peak = (tail[3:4] + tail[4:5]) + tail[5:6]
    return state[:HD].astype(f32), total, peak


def combined(a, b):
    sums_a, total_a, peak_a = a
    sums_b, total_b, peak_b = b
    peak = jnp.maximum(peak_a, peak_b)
    fold_a = jnp.exp2(peak_a - peak)
    fold_b = jnp.exp2(peak_b - peak)
    return sums_a * fold_a + sums_b * fold_b, total_a * fold_a + total_b * fold_b, peak


def open_state(state):
    tail = state[:, HD:].astype(f32)
    total = (tail[:, 0:1] + tail[:, 1:2]) + tail[:, 2:3]
    peak = (tail[:, 3:4] + tail[:, 4:5]) + tail[:, 5:6]
    return state[:, :HD].astype(f32), total, peak


def rounded(x):
    return lax.reduce_precision(x, 8, 7)


def closed_state(sums, total, peak):
    parts = [sums]
    for x in (total, peak):
        hi = rounded(x)
        mid = rounded(x - hi)
        parts += [hi, mid, rounded((x - hi) - mid)]
    parts.append(jnp.zeros((sums.shape[0], HR - HD - 6, sums.shape[2]), f32))
    return jnp.concatenate(parts, 1).astype(bf16)


def merged(states):
    states = [open_state(x) for x in states]
    while len(states) > 1:
        states = [combined(*states[n : n + 2]) for n in range(0, len(states), 2)]
    return states[0]


def out_kernel(*refs):
    parts, (wo_ref, gain_ref, out_ref, all_ref, done_ref, sems) = refs[:HEADS], refs[HEADS:]
    half, place = HEADS // 2, places()
    for t in range(HEADS):
        value = parts[t][0]
        h = (t % half) ^ place[t // half]
        all_ref[pl.ds(pl.multiple_of(h * HD, HD), HD), :] = value.astype(f32)
    attended = jnp.transpose(all_ref[...]).astype(bf16)
    lat = attended.shape[0]
    step = lat // 4
    copies = []
    for n in range(4):
        at = slice(n * step, (n + 1) * step)
        mixed = jnp.dot(attended[at], wo_ref[...], preferred_element_type=f32)
        done_ref[at] = rows_norm(mixed, 1) * gain_ref[...]
        copies.append(pltpu.make_async_copy(done_ref.at[at], out_ref.at[at], sems.at[n]))
        copies[-1].start()
    for copy in copies:
        copy.wait()


def shards(
    field, stem_weight, stem_bias, token_gain, kv_weight, latents,
    latent_gain, query_weight, head_gain, out_weight, out_gain,
):
    chan, rows, cols = field.shape
    width = stem_weight.shape[1]
    lat = latents.shape[0]
    nlat = lax.axis_size("lat")
    nlon = lax.axis_size("lon")
    half = cols // 2
    trows = rows // 2

    ahead = [(i, (i + 1) % nlon) for i in range(nlon)]
    back = [(t, s) for s, t in ahead]

    edge = shape((rows, 128), bf16)
    line = shape((CP, cols), bf16)
    first, last, low, high = call(
        edges_kernel, [edge, edge, line, line], 1, scratch=[VMEM((2, CP, cols), f32)]
    )(field)
    hl = lax.ppermute(last, "lon", ahead)
    hr = lax.ppermute(first, "lon", back)
    def framed(line, r):
        corners = [jnp.pad(h[r : r + 1], ((0, 0), (0, cols - 128))) for h in (hl, hr)]
        return jnp.concatenate([line[:CORNER]] + corners + [line[CORNER + 2 :]])

    low, high = framed(low, 0), framed(high, rows - 1)
    low, high, latents, hl, stem_weight, kv_weight = lax.optimization_barrier(
        (low, high, latents, hl, stem_weight, kv_weight)
    )
    up = [(i, i + 1) for i in range(nlat - 1)]
    down = [(t, s) for s, t in up]
    top = lax.ppermute(high, "lat", up)
    bot = lax.ppermute(low, "lat", down)
    qz = call(query_kernel, shape((HEADS, 4 * HD, lat), bf16), 3, smem=1)(
        head_gain, latents, latent_gain[None, :], query_weight
    )

    wt, wvt = call(
        weights_kernel,
        [shape((width, 16 * CP), bf16), shape((width, width), bf16)],
        2,
        scratch=[VMEM((16 * CP, width), f32)],
    )(stem_weight, kv_weight)
    patches = shape((rows + 2, 4 * CP, half), bf16)
    xs = call(
        select_kernel,
        patches,
        3,
        scratch=[VMEM((rows, CP, cols), bf16), VMEM((2, 128, 128), f32)],
    )(field, hl, hr)
    state = shape((HEADS // 2, HR, lat), bf16)
    tok, keep, send, _ = call(
        encode_kernel,
        [shape((trows, half, width), bf16), state, state, patches],
        9,
        out_spaces=[pl.ANY, VMEM, VMEM, VMEM],
        aliases={0: 3},
        scratch=encode_scratch(rows, cols, width, lat),
    )(xs, top, bot, wt, stem_bias[None, :], token_gain[None, :], kv_weight, wvt, qz)

    def swap(x, flips0, flips1):
        pairs = []
        for a in range(nlat):
            for b in range(nlon):
                to = {"lat": a, "lon": b}
                for axis, bit in flips1 if b & 1 else flips0:
                    to[axis] ^= bit
                pairs.append((a * nlon + b, to["lat"] * nlon + to["lon"]))
        return lax.ppermute(x, ("lat", "lon"), pairs)

    def subsets(bits):
        return [[bit for n, bit in enumerate(bits) if m >> n & 1] for m in range(1, 1 << len(bits))]

    cores = [("lon", 1)]
    first, second = ("lon", 2), ("lat", 1)
    near = list(zip(subsets([second, first]), subsets([first, second])))
    far = [("lat", 1 << n) for n in range(1, nlat.bit_length() - 1)]
    far += [("lon", 1 << n) for n in range(2, nlon.bit_length() - 1)]
    groups = [far[n : n + 2] for n in range(0, len(far), 2)]

    four = closed_state(*merged([keep, swap(send, cores, cores)]))
    own, *others = (four[n : n + 1] for n in range(HEADS // 2))
    states = [own] + [swap(x, *flips) for x, flips in zip(others, near)]
    for bits in groups:
        own = closed_state(*merged(states))
        states = [own] + [swap(own, flips, flips) for flips in subsets(bits)]
    sums, total, _ = merged(states)
    own = (sums / total).astype(bf16)
    parts = [own] + [swap(own, *flips) for flips in near]
    parts += [swap(x, cores, cores) for x in parts]
    latent_out = call(
        out_kernel,
        shape((lat, width), f32),
        HEADS + 2,
        out_spaces=[pl.ANY],
        scratch=[VMEM((width, lat), f32), VMEM((lat, width), f32), pltpu.SemaphoreType.DMA((4,))],
    )(*parts, out_weight, out_gain[None, :])
    return (tok, latent_out)


def solution(mesh):
    return jax.shard_map(
        shards,
        mesh=mesh,
        in_specs=(P(None, "lat", "lon"), P(), P(), P(), P(), P(), P(), P(), P(), P(), P()),
        out_specs=(P("lat", "lon", None), P()),
        check_vma=False,
    )
```

```python
import functools

import jax
import jax.numpy as jnp
from jax import lax
from jax.experimental import pallas as pl
from jax.experimental.pallas import tpu as pltpu
from jax.sharding import PartitionSpec as P

HEADS = 8
HD = 64
CP = 80
HR = 80
CT = 1024
VMEM = pltpu.VMEM
bf16 = jnp.bfloat16
f32 = jnp.float32
LIMIT = 44 << 20
CORNER = CP - 8
LOG2E = 1.4426950408889634


def call(kernel, out, n_in, scratch=(), smem=0, out_spaces=None, aliases=None, space=VMEM):
    outs = out if isinstance(out, (list, tuple)) else [out]
    spaces = out_spaces or [VMEM] * len(outs)
    specs = [pl.BlockSpec(memory_space=s) for s in spaces]
    kept = [VMEM(o.shape, o.dtype) if s is VMEM else o for o, s in zip(outs, spaces)]
    single = not isinstance(out, (list, tuple))
    fn = pl.pallas_call(
        kernel,
        out_shape=kept[0] if single else kept,
        in_specs=[pl.BlockSpec(memory_space=pltpu.SMEM)] * smem
        + [pl.BlockSpec(memory_space=space)] * n_in,
        out_specs=specs[0] if single else specs,
        scratch_shapes=list(scratch),
        input_output_aliases=aliases or {},
        compiler_params=pltpu.CompilerParams(vmem_limit_bytes=LIMIT),
    )

    def run(*args):
        held = [pltpu.with_memory_space_constraint(x, space) for x in args[smem:]]
        return fn(*args[:smem], *held)

    return run


def shape(dims, dtype):
    return jax.ShapeDtypeStruct(tuple(dims), dtype)


def rows_norm(x, axis):
    mean = jnp.mean(x, axis=axis, keepdims=True)
    centred = x - mean
    spread = jnp.mean(centred * centred, axis=axis, keepdims=True)
    return centred * lax.rsqrt(spread + 1e-05)


def split3(x):
    hi = x.astype(bf16)
    rest = x - hi.astype(f32)
    mid = rest.astype(bf16)
    lo = (rest - mid.astype(f32)).astype(bf16)
    return hi, mid, lo


def weights_kernel(w_ref, kv_ref, wt_ref, wvt_ref, pad_ref):
    chan = w_ref.shape[0] // 16
    width = w_ref.shape[1]
    for k in range(16):
        pad_ref[(k + 1) * CP - 16 : (k + 1) * CP] = jnp.zeros((16, width), f32)
        pad_ref[k * CP : k * CP + chan] = w_ref[k * chan : (k + 1) * chan].astype(f32)
    for k in range(0, 16 * CP, 256):
        wt_ref[:, k : k + 256] = jnp.transpose(pad_ref[k : k + 256].astype(bf16))
    wvt_ref[...] = jnp.transpose(kv_ref[:, width:])


def query_kernel(gain_ref, latents_ref, lgain_ref, qw_ref, qz_ref):
    normed = (rows_norm(latents_ref[...], 1) * lgain_ref[...]).astype(bf16)
    query = jnp.dot(normed, qw_ref[...], preferred_element_type=f32).astype(bf16)
    qt = jnp.transpose(query.astype(f32))
    zero = jnp.zeros((HD, qt.shape[1]), bf16)
    for h in range(HEADS):
        scaled = qt[h * HD : (h + 1) * HD] * (gain_ref[h] * (LOG2E / HD**0.5))
        hi = scaled.astype(bf16)
        lo = (scaled - hi.astype(f32)).astype(bf16)
        parts = [hi, zero, lo, zero] if h % 2 == 0 else [zero, hi, zero, lo]
        for j, part in enumerate(parts):
            qz_ref[h, j * HD : (j + 1) * HD, :] = part


def places():
    lon, lat = lax.axis_index("lon"), lax.axis_index("lat")
    core, by, bx = lon & 1, (lon >> 1) & 1, lat & 1
    yx, xy = 2 * by + bx, 2 * bx + by
    return 4 * core + yx + core * (xy - yx), 4 * (1 - core) + xy + core * (yx - xy)


def columns_kernel(x_ref, first_ref, last_ref, tile_ref, sems):
    chan, rows, cols = x_ref.shape
    lane = lax.broadcasted_iota(jnp.int32, (rows, 128), 1)
    ends = ((last_ref, cols - 128, 127), (first_ref, 0, 0))
    copies = [
        pltpu.make_async_copy(x_ref.at[:, :, at : at + 128], tile_ref.at[n], sems.at[n])
        for n, (_, at, _) in enumerate(ends)
    ]
    for copy in copies:
        copy.start()
    for n, (out_ref, _, c) in enumerate(ends):
        copies[n].wait()
        side = jnp.zeros((rows, 128), f32)
        for ch in range(chan):
            side = jnp.where(lane == ch, tile_ref[n, ch].astype(f32)[:, c : c + 1], side)
        out_ref[...] = side.astype(bf16)


def lines_kernel(x_ref, low_ref, high_ref, row_ref):
    chan, rows, cols = x_ref.shape
    row_ref[...] = jnp.zeros(row_ref.shape, f32)
    for ch in range(chan):
        row_ref[0, ch : ch + 1, :] = x_ref[ch, :16, :].astype(f32)[:1]
        row_ref[1, ch : ch + 1, :] = x_ref[ch, rows - 16 :, :].astype(f32)[15:]
    low_ref[...] = row_ref[0].astype(bf16)
    high_ref[...] = row_ref[1].astype(bf16)


def selection(cols):
    ci = lax.broadcasted_iota(jnp.int32, (cols, cols), 0)
    cj = lax.broadcasted_iota(jnp.int32, (cols, cols), 1)
    want = jnp.where(cj < cols // 2, 2 * cj, 2 * (cj - cols // 2) + 1)
    return jnp.where(ci == want, 1.0, 0.0).astype(bf16)


def spread(pair, select, xs_ref, where, sides):
    half = select.shape[0] // 2
    lane = lax.broadcasted_iota(jnp.int32, (CP, half), 1)
    sel = jnp.dot(pair, select, preferred_element_type=f32)
    for q, (left, right) in enumerate(sides):
        even = sel[q * CP : (q + 1) * CP, :half]
        odd = sel[q * CP : (q + 1) * CP, half:]
        first = jnp.where(lane == 0, left, pltpu.roll(odd, 1, 1))
        last = jnp.where(lane == half - 1, right, pltpu.roll(even, half - 1, 1))
        for kx, v in enumerate((first, even, odd, last)):
            xs_ref[where[q], kx * CP : (kx + 1) * CP, :] = v.astype(bf16)


def turned(ref, side_ref):
    side_ref[...] = jnp.zeros(side_ref.shape, f32)
    side_ref[: ref.shape[0]] = ref[...].astype(f32)
    return jnp.transpose(side_ref[...])[:CP]


def select_kernel(x_ref, hl_ref, hr_ref, xs_ref, y_ref, side_ref):
    chan, rows, cols = x_ref.shape

    i = lax.broadcasted_iota(jnp.int32, (256, 256), 0)
    j = lax.broadcasted_iota(jnp.int32, (256, 256), 1)
    perm = jnp.where(((i >> 4) == (j & 15)) & ((i & 15) == (j >> 4)), 1.0, 0.0).astype(bf16)
    for b in range(rows // 16):
        for g in range(CP // 16):
            n = min(16, chan - 16 * g)
            x = x_ref[16 * g : 16 * g + n, 16 * b : 16 * b + 16, :].reshape(n * 16, cols)
            y = jnp.dot(perm[:, : n * 16], x, preferred_element_type=f32).astype(bf16)
            y_ref[16 * b : 16 * b + 16, 16 * g : 16 * g + 16, :] = y.reshape(16, 16, cols)

    select = selection(cols)
    left, right = turned(hl_ref, side_ref.at[0]), turned(hr_ref, side_ref.at[1])
    for r in range(0, rows, 2):
        pair = y_ref[r : r + 2].reshape(2 * CP, cols)
        sides = [(left[:, q : q + 1], right[:, q : q + 1]) for q in (r, r + 1)]
        spread(pair, select, xs_ref, (r + 1, r + 2), sides)


def encode_kernel(
    xs_in, near_ref, far_ref, wt_ref, bias_ref, gain_ref, kv_ref, wvt_ref, qz_ref,
    tok_out, keep_ref, send_ref, xs_ref,
    st_ref, tok_ref, k_ref, vt_ref, s_ref, col_ref, state_ref, peak_ref, side_ref, sems,
):
    trows, half, width = tok_ref.shape
    rows, cols = 2 * trows, 2 * half
    tokens = trows * half
    lat = qz_ref.shape[2]

    odd = lax.axis_index("lat") & 1
    near, far = near_ref[...].astype(f32), far_ref[...].astype(f32)
    ends = (jnp.where(odd == 1, near, far), jnp.where(odd == 1, far, near))
    pair = jnp.concatenate(ends).astype(bf16)
    sides = []
    for n, end in enumerate(ends):
        corners = turned(end[CP - 16 :, :128], side_ref.at[n])
        at = CORNER - (CP - 16)
        sides.append((corners[:, at : at + 1], corners[:, at + 1 : at + 2]))
    spread(pair, selection(cols), xs_ref, (0, rows + 1), sides)

    for h in range(HEADS):
        vt_ref[h * HR + HD : (h + 1) * HR, :] = jnp.ones((HR - HD, tokens), bf16)

    for n, row in enumerate((bias_ref, gain_ref)):
        col_ref[n] = jnp.transpose(jnp.broadcast_to(row[...], (128, width)))

    def column(n):
        return jnp.concatenate([col_ref[n]] * (half // 128), axis=1)

    def stem(r, slot):
        patch = xs_ref[pl.ds(2 * r, 4)].reshape(16 * CP, half)
        st_ref[slot] = jnp.dot(wt_ref[...], patch, preferred_element_type=f32)

    def finish(r, slot):
        value = rows_norm(st_ref[slot] + column(0), 0) * column(1)
        tt = value.astype(bf16)
        tok = jnp.transpose(tt)
        tok_ref[r] = tok
        pltpu.make_async_copy(tok_ref.at[r], tok_out.at[r], sems.at[r]).start()
        at = pl.ds(pl.multiple_of(r * half, half), half)
        k_ref[at, :] = jnp.dot(tok, kv_ref[:, :width], preferred_element_type=f32).astype(bf16)
        vt = jnp.dot(wvt_ref[...], tt, preferred_element_type=f32).astype(bf16)
        for h in range(HEADS):
            vt_ref[h * HR : h * HR + HD, at] = vt[h * HD : (h + 1) * HD]

    stem(0, 0)

    def band(n, carry):
        r = 2 * n
        stem(r + 1, 1)
        finish(r, 0)
        stem(jnp.minimum(r + 2, trows - 1), 0)
        finish(r + 1, 1)
        return carry

    lax.fori_loop(0, trows // 2, band, 0)

    def produce(h, c, slot):
        pair = pl.ds(pl.multiple_of((h >> 1) * (2 * HD), 2 * HD), 2 * HD)
        keys = k_ref[c * CT : (c + 1) * CT, pair]
        keys = jnp.concatenate([keys, keys], axis=1)
        s = jnp.dot(keys, qz_ref[h], preferred_element_type=f32)
        s_ref[slot] = s
        return jnp.max(s, axis=0, keepdims=True)

    chunks = tokens // CT
    mine, other = places()

    def head_of(t):
        late = t >> (HEADS.bit_length() - 2)
        return (t & (HEADS // 2 - 1)) ^ (mine + late * (other - mine))

    def head(t, most):
        h = head_of(t)
        after = head_of(jnp.minimum(t + 1, HEADS - 1))
        peak = jnp.full((1, lat), -1e30, f32)
        state = jnp.zeros((HR, lat), f32)
        for c in range(chunks):
            if c + 1 < chunks:
                following = produce(h, c + 1, (c + 1) % 2)
            else:
                following = produce(after, 0, (c + 1) % 2)
            newpeak = jnp.maximum(peak, jnp.ceil(most))
            fold = jnp.exp2(peak - newpeak)
            weights = jnp.exp2(s_ref[c % 2] - newpeak).astype(bf16)
            values = vt_ref[pl.ds(pl.multiple_of(h * HR, 16), HR), c * CT : (c + 1) * CT]
            state = state * fold + jnp.dot(values, weights, preferred_element_type=f32)
            peak, most = newpeak, following
        state_ref[t] = state
        peak_ref[t] = peak
        return most

    lax.fori_loop(0, HEADS, head, produce(head_of(0), 0, 0))
    for t in range(HEADS):
        state = state_ref[t]
        packed = pack(state[:HD], state[HD : HD + 1], peak_ref[t])
        (keep_ref if t < HEADS // 2 else send_ref)[t % (HEADS // 2)] = packed
    for r in range(trows):
        pltpu.make_async_copy(tok_ref.at[r], tok_out.at[r], sems.at[r]).wait()


def encode_scratch(rows, cols, width, lat):
    half, trows = cols // 2, rows // 2
    tokens = trows * half
    return [
        VMEM((2, width, half), f32),
        VMEM((trows, half, width), bf16),
        VMEM((tokens, width), bf16),
        VMEM((HEADS * HR, tokens), bf16),
        VMEM((2, CT, lat), f32),
        VMEM((2, width, 128), f32),
        VMEM((HEADS, HR, lat), f32),
        VMEM((HEADS, 1, lat), f32),
        VMEM((2, 128, 128), f32),
        pltpu.SemaphoreType.DMA((trows,)),
    ]


def pack(sums, total, peak):
    lat = sums.shape[1]
    row = lax.broadcasted_iota(jnp.int32, (16, lat), 0)
    tail = jnp.zeros((16, lat), f32)
    for n, part in enumerate(split3(total) + split3(peak)):
        tail = jnp.where(row == n, part.astype(f32), tail)
    return jnp.concatenate([sums.astype(bf16), tail.astype(bf16)], axis=0)


def unpack(state):
    tail = state[HD:].astype(f32)
    total = (tail[0:1] + tail[1:2]) + tail[2:3]
    peak = (tail[3:4] + tail[4:5]) + tail[5:6]
    return state[:HD].astype(f32), total, peak


def combined(a, b):
    sums_a, total_a, peak_a = a
    sums_b, total_b, peak_b = b
    peak = jnp.maximum(peak_a, peak_b)
    fold_a = jnp.exp2(peak_a - peak)
    fold_b = jnp.exp2(peak_b - peak)
    return sums_a * fold_a + sums_b * fold_b, total_a * fold_a + total_b * fold_b, peak


def open_state(state):
    tail = state[:, HD:].astype(f32)
    total = (tail[:, 0:1] + tail[:, 1:2]) + tail[:, 2:3]
    peak = (tail[:, 3:4] + tail[:, 4:5]) + tail[:, 5:6]
    return state[:, :HD].astype(f32), total, peak


def rounded(x):
    return lax.reduce_precision(x, 8, 7)


def closed_state(sums, total, peak):
    parts = [sums]
    for x in (total, peak):
        hi = rounded(x)
        mid = rounded(x - hi)
        parts += [hi, mid, rounded((x - hi) - mid)]
    parts.append(jnp.zeros((sums.shape[0], HR - HD - 6, sums.shape[2]), f32))
    return jnp.concatenate(parts, 1).astype(bf16)


def merged(states):
    states = [open_state(x) for x in states]
    while len(states) > 1:
        states = [combined(*states[n : n + 2]) for n in range(0, len(states), 2)]
    return states[0]


def out_kernel(*refs):
    parts, (wo_ref, gain_ref, out_ref, all_ref, done_ref, sems) = refs[:HEADS], refs[HEADS:]
    half, place = HEADS // 2, places()
    for t in range(HEADS):
        value = parts[t][0]
        h = (t % half) ^ place[t // half]
        all_ref[pl.ds(pl.multiple_of(h * HD, HD), HD), :] = value.astype(f32)
    attended = jnp.transpose(all_ref[...]).astype(bf16)
    lat = attended.shape[0]
    step = lat // 4
    copies = []
    for n in range(4):
        at = slice(n * step, (n + 1) * step)
        mixed = jnp.dot(attended[at], wo_ref[...], preferred_element_type=f32)
        done_ref[at] = rows_norm(mixed, 1) * gain_ref[...]
        copies.append(pltpu.make_async_copy(done_ref.at[at], out_ref.at[at], sems.at[n]))
        copies[-1].start()
    for copy in copies:
        copy.wait()


def shards(
    field, stem_weight, stem_bias, token_gain, kv_weight, latents,
    latent_gain, query_weight, head_gain, out_weight, out_gain,
):
    chan, rows, cols = field.shape
    width = stem_weight.shape[1]
    lat = latents.shape[0]
    nlat = lax.axis_size("lat")
    nlon = lax.axis_size("lon")
    half = cols // 2
    trows = rows // 2

    ahead = [(i, (i + 1) % nlon) for i in range(nlon)]
    back = [(t, s) for s, t in ahead]

    edge = shape((rows, 128), bf16)
    line = shape((CP, cols), bf16)
    first, last = call(
        columns_kernel,
        [edge, edge],
        1,
        space=pltpu.HBM,
        scratch=[VMEM((2, chan, rows, 128), bf16), pltpu.SemaphoreType.DMA((2,))],
    )(field)
    low, high = call(lines_kernel, [line, line], 1, scratch=[VMEM((2, CP, cols), f32)])(field)
    hl = lax.ppermute(last, "lon", ahead)
    hr = lax.ppermute(first, "lon", back)
    def framed(line, r):
        corners = [jnp.pad(h[r : r + 1], ((0, 0), (0, cols - 128))) for h in (hl, hr)]
        return jnp.concatenate([line[:CORNER]] + corners + [line[CORNER + 2 :]])

    low, high = framed(low, 0), framed(high, rows - 1)
    low, high, latents, hl, stem_weight, kv_weight = lax.optimization_barrier(
        (low, high, latents, hl, stem_weight, kv_weight)
    )
    odd = (lax.axis_index("lat") & 1) == 1
    twos = [(i, i ^ 1) for i in range(nlat) if i ^ 1 < nlat]
    others = [(i, ((i + 1) ^ 1) - 1) for i in range(nlat)]
    others = [(i, j) for i, j in others if 0 <= j < nlat]
    near_row = lax.ppermute(jnp.where(odd, low, high), "lat", twos)
    far_row = lax.ppermute(jnp.where(odd, high, low), "lat", others)
    qz = call(query_kernel, shape((HEADS, 4 * HD, lat), bf16), 3, smem=1)(
        head_gain, latents, latent_gain[None, :], query_weight
    )
    wt, wvt = call(
        weights_kernel,
        [shape((width, 16 * CP), bf16), shape((width, width), bf16)],
        2,
        scratch=[VMEM((16 * CP, width), f32)],
    )(stem_weight, kv_weight)
    patches = shape((rows + 2, 4 * CP, half), bf16)
    xs = call(
        select_kernel,
        patches,
        3,
        scratch=[VMEM((rows, CP, cols), bf16), VMEM((2, 128, 128), f32)],
    )(field, hl, hr)
    state = shape((HEADS // 2, HR, lat), bf16)
    tok, keep, send, _ = call(
        encode_kernel,
        [shape((trows, half, width), bf16), state, state, patches],
        9,
        out_spaces=[pl.ANY, VMEM, VMEM, VMEM],
        aliases={0: 3},
        scratch=encode_scratch(rows, cols, width, lat),
    )(xs, near_row, far_row, wt, stem_bias[None, :], token_gain[None, :], kv_weight, wvt, qz)

    def swap(x, flips0, flips1):
        pairs = []
        for a in range(nlat):
            for b in range(nlon):
                to = {"lat": a, "lon": b}
                for axis, bit in flips1 if b & 1 else flips0:
                    to[axis] ^= bit
                pairs.append((a * nlon + b, to["lat"] * nlon + to["lon"]))
        return lax.ppermute(x, ("lat", "lon"), pairs)

    def subsets(bits):
        return [[bit for n, bit in enumerate(bits) if m >> n & 1] for m in range(1, 1 << len(bits))]

    cores = [("lon", 1)]
    first, second = ("lon", 2), ("lat", 1)
    near = list(zip(subsets([second, first]), subsets([first, second])))
    far = [("lat", 1 << n) for n in range(1, nlat.bit_length() - 1)]
    far += [("lon", 1 << n) for n in range(2, nlon.bit_length() - 1)]
    groups = [far[n : n + 2] for n in range(0, len(far), 2)]

    four = closed_state(*merged([keep, swap(send, cores, cores)]))
    own, *others = (four[n : n + 1] for n in range(HEADS // 2))
    states = [own] + [swap(x, *flips) for x, flips in zip(others, near)]
    for bits in groups:
        own = closed_state(*merged(states))
        states = [own] + [swap(own, flips, flips) for flips in subsets(bits)]
    sums, total, _ = merged(states)
    own = (sums / total).astype(bf16)
    parts = [own] + [swap(own, *flips) for flips in near]
    parts += [swap(x, cores, cores) for x in parts]
    latent_out = call(
        out_kernel,
        shape((lat, width), f32),
        HEADS + 2,
        out_spaces=[pl.ANY],
        scratch=[VMEM((width, lat), f32), VMEM((lat, width), f32), pltpu.SemaphoreType.DMA((4,))],
    )(*parts, out_weight, out_gain[None, :])
    return (tok, latent_out)


def solution(mesh):
    return jax.shard_map(
        shards,
        mesh=mesh,
        in_specs=(P(None, "lat", "lon"), P(), P(), P(), P(), P(), P(), P(), P(), P(), P()),
        out_specs=(P("lat", "lon", None), P()),
        check_vma=False,
    )
```

```python
import functools

import jax
import jax.numpy as jnp
from jax import lax
from jax.experimental import pallas as pl
from jax.experimental.pallas import tpu as pltpu
from jax.sharding import PartitionSpec as P

HEADS = 8
HD = 64
CP = 80
HR = 80
CT = 1024
VMEM = pltpu.VMEM
bf16 = jnp.bfloat16
f32 = jnp.float32
LIMIT = 44 << 20
CORNER = CP - 8
LOG2E = 1.4426950408889634


def call(kernel, out, n_in, scratch=(), smem=0, out_spaces=None, aliases=None, space=VMEM):
    outs = out if isinstance(out, (list, tuple)) else [out]
    spaces = out_spaces or [VMEM] * len(outs)
    specs = [pl.BlockSpec(memory_space=s) for s in spaces]
    kept = [VMEM(o.shape, o.dtype) if s is VMEM else o for o, s in zip(outs, spaces)]
    single = not isinstance(out, (list, tuple))
    fn = pl.pallas_call(
        kernel,
        out_shape=kept[0] if single else kept,
        in_specs=[pl.BlockSpec(memory_space=pltpu.SMEM)] * smem
        + [pl.BlockSpec(memory_space=space)] * n_in,
        out_specs=specs[0] if single else specs,
        scratch_shapes=list(scratch),
        input_output_aliases=aliases or {},
        compiler_params=pltpu.CompilerParams(vmem_limit_bytes=LIMIT),
    )

    def run(*args):
        held = [pltpu.with_memory_space_constraint(x, space) for x in args[smem:]]
        return fn(*args[:smem], *held)

    return run


def shape(dims, dtype):
    return jax.ShapeDtypeStruct(tuple(dims), dtype)


def rows_norm(x, axis):
    mean = jnp.mean(x, axis=axis, keepdims=True)
    centred = x - mean
    spread = jnp.mean(centred * centred, axis=axis, keepdims=True)
    return centred * lax.rsqrt(spread + 1e-05)


def split3(x):
    hi = x.astype(bf16)
    rest = x - hi.astype(f32)
    mid = rest.astype(bf16)
    lo = (rest - mid.astype(f32)).astype(bf16)
    return hi, mid, lo


def weights_kernel(w_ref, kv_ref, wt_ref, wvt_ref, pad_ref):
    chan = w_ref.shape[0] // 16
    width = w_ref.shape[1]
    for k in range(16):
        pad_ref[(k + 1) * CP - 16 : (k + 1) * CP] = jnp.zeros((16, width), f32)
        pad_ref[k * CP : k * CP + chan] = w_ref[k * chan : (k + 1) * chan].astype(f32)
    for k in range(0, 16 * CP, 256):
        wt_ref[:, k : k + 256] = jnp.transpose(pad_ref[k : k + 256].astype(bf16))
    wvt_ref[...] = jnp.transpose(kv_ref[:, width:])


def query_kernel(gain_ref, latents_ref, lgain_ref, qw_ref, qz_ref):
    normed = (rows_norm(latents_ref[...], 1) * lgain_ref[...]).astype(bf16)
    query = jnp.dot(normed, qw_ref[...], preferred_element_type=f32).astype(bf16)
    qt = jnp.transpose(query.astype(f32))
    zero = jnp.zeros((HD, qt.shape[1]), bf16)
    for h in range(HEADS):
        scaled = qt[h * HD : (h + 1) * HD] * (gain_ref[h] * (LOG2E / HD**0.5))
        hi = scaled.astype(bf16)
        lo = (scaled - hi.astype(f32)).astype(bf16)
        parts = [hi, zero, lo, zero] if h % 2 == 0 else [zero, hi, zero, lo]
        for j, part in enumerate(parts):
            qz_ref[h, j * HD : (j + 1) * HD, :] = part


def places():
    lon, lat = lax.axis_index("lon"), lax.axis_index("lat")
    core, by, bx = lon & 1, (lon >> 1) & 1, lat & 1
    yx, xy = 2 * by + bx, 2 * bx + by
    return 4 * core + yx + core * (xy - yx), 4 * (1 - core) + xy + core * (yx - xy)


def columns_kernel(x_ref, first_ref, last_ref, tile_ref, sems):
    chan, rows, cols = x_ref.shape
    lane = lax.broadcasted_iota(jnp.int32, (rows, 128), 1)
    ends = ((last_ref, cols - 128, 127), (first_ref, 0, 0))
    copies = [
        pltpu.make_async_copy(x_ref.at[:, :, at : at + 128], tile_ref.at[n], sems.at[n])
        for n, (_, at, _) in enumerate(ends)
    ]
    for copy in copies:
        copy.start()
    for n, (out_ref, _, c) in enumerate(ends):
        copies[n].wait()
        side = jnp.zeros((rows, 128), f32)
        for ch in range(chan):
            side = jnp.where(lane == ch, tile_ref[n, ch].astype(f32)[:, c : c + 1], side)
        out_ref[...] = side.astype(bf16)


def lines_kernel(x_ref, low_ref, high_ref, row_ref):
    chan, rows, cols = x_ref.shape
    row_ref[...] = jnp.zeros(row_ref.shape, f32)
    for ch in range(chan):
        row_ref[0, ch : ch + 1, :] = x_ref[ch, :16, :].astype(f32)[:1]
        row_ref[1, ch : ch + 1, :] = x_ref[ch, rows - 16 :, :].astype(f32)[15:]
    low_ref[...] = row_ref[0].astype(bf16)
    high_ref[...] = row_ref[1].astype(bf16)


def selection(cols):
    ci = lax.broadcasted_iota(jnp.int32, (cols, cols), 0)
    cj = lax.broadcasted_iota(jnp.int32, (cols, cols), 1)
    want = jnp.where(cj < cols // 2, 2 * cj, 2 * (cj - cols // 2) + 1)
    return jnp.where(ci == want, 1.0, 0.0).astype(bf16)


def spread(pair, select, xs_ref, where, sides):
    half = select.shape[0] // 2
    lane = lax.broadcasted_iota(jnp.int32, (CP, half), 1)
    sel = jnp.dot(pair, select, preferred_element_type=f32)
    for q, (left, right) in enumerate(sides):
        even = sel[q * CP : (q + 1) * CP, :half]
        odd = sel[q * CP : (q + 1) * CP, half:]
        first = jnp.where(lane == 0, left, pltpu.roll(odd, 1, 1))
        last = jnp.where(lane == half - 1, right, pltpu.roll(even, half - 1, 1))
        for kx, v in enumerate((first, even, odd, last)):
            xs_ref[where[q], kx * CP : (kx + 1) * CP, :] = v.astype(bf16)


def turned(ref, side_ref):
    side_ref[...] = jnp.zeros(side_ref.shape, f32)
    side_ref[: ref.shape[0]] = ref[...].astype(f32)
    return jnp.transpose(side_ref[...])[:CP]


def select_kernel(x_ref, hl_ref, hr_ref, xs_ref, y_ref, side_ref):
    chan, rows, cols = x_ref.shape

    i = lax.broadcasted_iota(jnp.int32, (256, 256), 0)
    j = lax.broadcasted_iota(jnp.int32, (256, 256), 1)
    perm = jnp.where(((i >> 4) == (j & 15)) & ((i & 15) == (j >> 4)), 1.0, 0.0).astype(bf16)
    for b in range(rows // 16):
        for g in range(CP // 16):
            n = min(16, chan - 16 * g)
            x = x_ref[16 * g : 16 * g + n, 16 * b : 16 * b + 16, :].reshape(n * 16, cols)
            y = jnp.dot(perm[:, : n * 16], x, preferred_element_type=f32).astype(bf16)
            y_ref[16 * b : 16 * b + 16, 16 * g : 16 * g + 16, :] = y.reshape(16, 16, cols)

    select = selection(cols)
    left, right = turned(hl_ref, side_ref.at[0]), turned(hr_ref, side_ref.at[1])
    for r in range(0, rows, 2):
        pair = y_ref[r : r + 2].reshape(2 * CP, cols)
        sides = [(left[:, q : q + 1], right[:, q : q + 1]) for q in (r, r + 1)]
        spread(pair, select, xs_ref, (r + 1, r + 2), sides)


def encode_kernel(
    xs_in, near_ref, far_ref, wt_ref, bias_ref, gain_ref, kv_ref, wvt_ref, qz_ref,
    tok_out, keep_ref, send_ref, xs_ref,
    st_ref, tok_ref, k_ref, vt_ref, s_ref, col_ref, state_ref, peak_ref, side_ref, sems,
):
    trows, half, width = tok_ref.shape
    rows, cols = 2 * trows, 2 * half
    tokens = trows * half
    lat = qz_ref.shape[2]

    odd = lax.axis_index("lat") & 1
    near, far = near_ref[...].astype(f32), far_ref[...].astype(f32)
    ends = (jnp.where(odd == 1, near, far), jnp.where(odd == 1, far, near))
    pair = jnp.concatenate(ends).astype(bf16)
    sides = []
    for n, end in enumerate(ends):
        corners = turned(end[CP - 16 :, :128], side_ref.at[n])
        at = CORNER - (CP - 16)
        sides.append((corners[:, at : at + 1], corners[:, at + 1 : at + 2]))
    spread(pair, selection(cols), xs_ref, (0, rows + 1), sides)

    for h in range(HEADS):
        vt_ref[h * HR + HD : (h + 1) * HR, :] = jnp.ones((HR - HD, tokens), bf16)

    for n, row in enumerate((bias_ref, gain_ref)):
        col_ref[n] = jnp.transpose(jnp.broadcast_to(row[...], (128, width)))

    def column(n):
        return jnp.concatenate([col_ref[n]] * (half // 128), axis=1)

    def stem(r, slot):
        patch = xs_ref[pl.ds(2 * r, 4)].reshape(16 * CP, half)
        st_ref[slot] = jnp.dot(wt_ref[...], patch, preferred_element_type=f32)

    def finish(r, slot):
        value = rows_norm(st_ref[slot] + column(0), 0) * column(1)
        tt = value.astype(bf16)
        tok = jnp.transpose(tt)
        tok_ref[r] = tok
        pltpu.make_async_copy(tok_ref.at[r], tok_out.at[r], sems.at[r]).start()
        at = pl.ds(pl.multiple_of(r * half, half), half)
        k_ref[at, :] = jnp.dot(tok, kv_ref[:, :width], preferred_element_type=f32).astype(bf16)
        vt = jnp.dot(wvt_ref[...], tt, preferred_element_type=f32).astype(bf16)
        for h in range(HEADS):
            vt_ref[h * HR : h * HR + HD, at] = vt[h * HD : (h + 1) * HD]

    stem(0, 0)

    def band(n, carry):
        r = 2 * n
        stem(r + 1, 1)
        finish(r, 0)
        stem(jnp.minimum(r + 2, trows - 1), 0)
        finish(r + 1, 1)
        return carry

    lax.fori_loop(0, trows // 2, band, 0, unroll=2)

    def produce(h, c, slot):
        pair = pl.ds(pl.multiple_of((h >> 1) * (2 * HD), 2 * HD), 2 * HD)
        keys = k_ref[c * CT : (c + 1) * CT, pair]
        keys = jnp.concatenate([keys, keys], axis=1)
        s = jnp.dot(keys, qz_ref[h], preferred_element_type=f32)
        s_ref[slot] = s
        return jnp.max(s, axis=0, keepdims=True)

    chunks = tokens // CT
    mine, other = places()

    def head_of(t):
        late = t >> (HEADS.bit_length() - 2)
        return (t & (HEADS // 2 - 1)) ^ (mine + late * (other - mine))

    def head(t, most):
        h = head_of(t)
        after = head_of(jnp.minimum(t + 1, HEADS - 1))
        peak = jnp.full((1, lat), -1e30, f32)
        state = jnp.zeros((HR, lat), f32)
        for c in range(chunks):
            if c + 1 < chunks:
                following = produce(h, c + 1, (c + 1) % 2)
            else:
                following = produce(after, 0, (c + 1) % 2)
            newpeak = jnp.maximum(peak, jnp.ceil(most))
            fold = jnp.exp2(peak - newpeak)
            weights = jnp.exp2(s_ref[c % 2] - newpeak).astype(bf16)
            values = vt_ref[pl.ds(pl.multiple_of(h * HR, 16), HR), c * CT : (c + 1) * CT]
            state = state * fold + jnp.dot(values, weights, preferred_element_type=f32)
            peak, most = newpeak, following
        state_ref[t] = state
        peak_ref[t] = peak
        return most

    lax.fori_loop(0, HEADS, head, produce(head_of(0), 0, 0))
    for t in range(HEADS):
        state = state_ref[t]
        packed = pack(state[:HD], state[HD : HD + 1], peak_ref[t])
        (keep_ref if t < HEADS // 2 else send_ref)[t % (HEADS // 2)] = packed
    for r in range(trows):
        pltpu.make_async_copy(tok_ref.at[r], tok_out.at[r], sems.at[r]).wait()


def encode_scratch(rows, cols, width, lat):
    half, trows = cols // 2, rows // 2
    tokens = trows * half
    return [
        VMEM((2, width, half), f32),
        VMEM((trows, half, width), bf16),
        VMEM((tokens, width), bf16),
        VMEM((HEADS * HR, tokens), bf16),
        VMEM((2, CT, lat), f32),
        VMEM((2, width, 128), f32),
        VMEM((HEADS, HR, lat), f32),
        VMEM((HEADS, 1, lat), f32),
        VMEM((2, 128, 128), f32),
        pltpu.SemaphoreType.DMA((trows,)),
    ]


def pack(sums, total, peak):
    lat = sums.shape[1]
    row = lax.broadcasted_iota(jnp.int32, (16, lat), 0)
    tail = jnp.zeros((16, lat), f32)
    for n, part in enumerate(split3(total) + split3(peak)):
        tail = jnp.where(row == n, part.astype(f32), tail)
    return jnp.concatenate([sums.astype(bf16), tail.astype(bf16)], axis=0)


def unpack(state):
    tail = state[HD:].astype(f32)
    total = (tail[0:1] + tail[1:2]) + tail[2:3]
    peak = (tail[3:4] + tail[4:5]) + tail[5:6]
    return state[:HD].astype(f32), total, peak


def combined(a, b):
    sums_a, total_a, peak_a = a
    sums_b, total_b, peak_b = b
    peak = jnp.maximum(peak_a, peak_b)
    fold_a = jnp.exp2(peak_a - peak)
    fold_b = jnp.exp2(peak_b - peak)
    return sums_a * fold_a + sums_b * fold_b, total_a * fold_a + total_b * fold_b, peak


def open_state(state):
    tail = state[:, HD:].astype(f32)
    total = (tail[:, 0:1] + tail[:, 1:2]) + tail[:, 2:3]
    peak = (tail[:, 3:4] + tail[:, 4:5]) + tail[:, 5:6]
    return state[:, :HD].astype(f32), total, peak


def rounded(x):
    return lax.reduce_precision(x, 8, 7)


def closed_state(sums, total, peak):
    parts = [sums]
    for x in (total, peak):
        hi = rounded(x)
        mid = rounded(x - hi)
        parts += [hi, mid, rounded((x - hi) - mid)]
    parts.append(jnp.zeros((sums.shape[0], HR - HD - 6, sums.shape[2]), f32))
    return jnp.concatenate(parts, 1).astype(bf16)


def merged(states):
    states = [open_state(x) for x in states]
    while len(states) > 1:
        states = [combined(*states[n : n + 2]) for n in range(0, len(states), 2)]
    return states[0]


def out_kernel(*refs):
    parts, (wo_ref, gain_ref, out_ref, all_ref, done_ref, sems) = refs[:HEADS], refs[HEADS:]
    half, place = HEADS // 2, places()
    for t in range(HEADS):
        value = parts[t][0]
        h = (t % half) ^ place[t // half]
        all_ref[pl.ds(pl.multiple_of(h * HD, HD), HD), :] = value.astype(f32)
    attended = jnp.transpose(all_ref[...]).astype(bf16)
    lat = attended.shape[0]
    step = lat // 4
    copies = []
    for n in range(4):
        at = slice(n * step, (n + 1) * step)
        mixed = jnp.dot(attended[at], wo_ref[...], preferred_element_type=f32)
        done_ref[at] = rows_norm(mixed, 1) * gain_ref[...]
        copies.append(pltpu.make_async_copy(done_ref.at[at], out_ref.at[at], sems.at[n]))
        copies[-1].start()
    for copy in copies:
        copy.wait()


def shards(
    field, stem_weight, stem_bias, token_gain, kv_weight, latents,
    latent_gain, query_weight, head_gain, out_weight, out_gain,
):
    chan, rows, cols = field.shape
    width = stem_weight.shape[1]
    lat = latents.shape[0]
    nlat = lax.axis_size("lat")
    nlon = lax.axis_size("lon")
    half = cols // 2
    trows = rows // 2

    ahead = [(i, (i + 1) % nlon) for i in range(nlon)]
    back = [(t, s) for s, t in ahead]

    edge = shape((rows, 128), bf16)
    line = shape((CP, cols), bf16)
    first, last = call(
        columns_kernel,
        [edge, edge],
        1,
        space=pltpu.HBM,
        scratch=[VMEM((2, chan, rows, 128), bf16), pltpu.SemaphoreType.DMA((2,))],
    )(field)
    low, high = call(lines_kernel, [line, line], 1, scratch=[VMEM((2, CP, cols), f32)])(field)
    hl = lax.ppermute(last, "lon", ahead)
    hr = lax.ppermute(first, "lon", back)
    def framed(line, r):
        corners = [jnp.pad(h[r : r + 1], ((0, 0), (0, cols - 128))) for h in (hl, hr)]
        return jnp.concatenate([line[:CORNER]] + corners + [line[CORNER + 2 :]])

    low, high = framed(low, 0), framed(high, rows - 1)
    low, high, latents, hl, stem_weight, kv_weight = lax.optimization_barrier(
        (low, high, latents, hl, stem_weight, kv_weight)
    )
    odd = (lax.axis_index("lat") & 1) == 1
    twos = [(i, i ^ 1) for i in range(nlat) if i ^ 1 < nlat]
    others = [(i, ((i + 1) ^ 1) - 1) for i in range(nlat)]
    others = [(i, j) for i, j in others if 0 <= j < nlat]
    near_row = lax.ppermute(jnp.where(odd, low, high), "lat", twos)
    far_row = lax.ppermute(jnp.where(odd, high, low), "lat", others)
    qz = call(query_kernel, shape((HEADS, 4 * HD, lat), bf16), 3, smem=1)(
        head_gain, latents, latent_gain[None, :], query_weight
    )
    wt, wvt = call(
        weights_kernel,
        [shape((width, 16 * CP), bf16), shape((width, width), bf16)],
        2,
        scratch=[VMEM((16 * CP, width), f32)],
    )(stem_weight, kv_weight)
    patches = shape((rows + 2, 4 * CP, half), bf16)
    xs = call(
        select_kernel,
        patches,
        3,
        scratch=[VMEM((rows, CP, cols), bf16), VMEM((2, 128, 128), f32)],
    )(field, hl, hr)
    state = shape((HEADS // 2, HR, lat), bf16)
    tok, keep, send, _ = call(
        encode_kernel,
        [shape((trows, half, width), bf16), state, state, patches],
        9,
        out_spaces=[pl.ANY, VMEM, VMEM, VMEM],
        aliases={0: 3},
        scratch=encode_scratch(rows, cols, width, lat),
    )(xs, near_row, far_row, wt, stem_bias[None, :], token_gain[None, :], kv_weight, wvt, qz)

    def swap(x, flips0, flips1):
        pairs = []
        for a in range(nlat):
            for b in range(nlon):
                to = {"lat": a, "lon": b}
                for axis, bit in flips1 if b & 1 else flips0:
                    to[axis] ^= bit
                pairs.append((a * nlon + b, to["lat"] * nlon + to["lon"]))
        return lax.ppermute(x, ("lat", "lon"), pairs)

    def subsets(bits):
        return [[bit for n, bit in enumerate(bits) if m >> n & 1] for m in range(1, 1 << len(bits))]

    cores = [("lon", 1)]
    first, second = ("lon", 2), ("lat", 1)
    near = list(zip(subsets([second, first]), subsets([first, second])))
    far = [("lat", 1 << n) for n in range(1, nlat.bit_length() - 1)]
    far += [("lon", 1 << n) for n in range(2, nlon.bit_length() - 1)]
    groups = [far[n : n + 2] for n in range(0, len(far), 2)]

    four = closed_state(*merged([keep, swap(send, cores, cores)]))
    own, *others = (four[n : n + 1] for n in range(HEADS // 2))
    states = [own] + [swap(x, *flips) for x, flips in zip(others, near)]
    for bits in groups:
        own = closed_state(*merged(states))
        states = [own] + [swap(own, flips, flips) for flips in subsets(bits)]
    sums, total, _ = merged(states)
    own = (sums / total).astype(bf16)
    parts = [own] + [swap(own, *flips) for flips in near]
    parts += [swap(x, cores, cores) for x in parts]
    latent_out = call(
        out_kernel,
        shape((lat, width), f32),
        HEADS + 2,
        out_spaces=[pl.ANY],
        scratch=[VMEM((width, lat), f32), VMEM((lat, width), f32), pltpu.SemaphoreType.DMA((4,))],
    )(*parts, out_weight, out_gain[None, :])
    return (tok, latent_out)


def solution(mesh):
    return jax.shard_map(
        shards,
        mesh=mesh,
        in_specs=(P(None, "lat", "lon"), P(), P(), P(), P(), P(), P(), P(), P(), P(), P()),
        out_specs=(P("lat", "lon", None), P()),
        check_vma=False,
    )
```
